32 devices in a mesh: facet: 4 (over y, x), team: 8 (over z, core).
Axes of the slice: x: 2, y: 2, z: 4, core: 2. Of those that a mesh axis runs over, the one named last changes fastest.
Arguments:
- facets: float32 [4, 2, 512, 5120], P('facet', None, 'team'), may hold values from -6 to 6
- facet_offsets: int32 [4], replicated, may hold values from 0 to 65535
- grid_offsets: int32 [8], replicated, may hold values from 0 to 65535
- taper: float32 [512], replicated, may hold values from 0.3 to 3
- kernels: float32 [16, 2, 512], replicated, may hold values from -4 to 4
- kernel_index: int32 [8, 512], P('facet', 'team'), may hold values from 0 to 15
- residual: float32 [8, 2, 512, 512], P('facet', None, 'team'), may hold values from -6 to 6
Outputs:
- facet_update: float32 [4, 2, 512, 5120], P('facet', None, 'team')
The draws below stay inside these ranges and needn't reach their ends.
All inputs are finite; a program needn't handle non-finite values.
Results may differ from the reference program's by a relative error of at most 0.0003.
Values sent between devices are 32-bit elements; how exact they have to be, the bound alone decides.
No kernel may reach another device: no remote copies, remote signals or barrier semaphores. Data moves between devices by JAX's collectives and lax.ppermute only.
A program may use at most 64 MiB of HBM per device.

```python
import math
import jax
import jax.numpy as jnp
from jax import lax

N_IMG = 65536
FACET_LEN = 5120
SUB = 512
KERNELS = 16
FACETS = 4
SUBGRIDS = 8


def with_ends(array, own_key, least, top_value):
    shape = array.shape
    spot = [jax.random.randint(jax.random.fold_in(own_key, axis), (), 0, shape[axis]) for axis in range(len(shape))]
    array = array.at[tuple(spot)].set(least)
    longest = shape.index(max(shape))
    spot[longest] = (spot[longest] + 1) % shape[longest]
    return array.at[tuple(spot)].set(top_value)


def steps_of(own_key, dims, split, low, high):
    gain, own = 1.0, jax.random.fold_in(own_key, 6)
    for dim, blocks in split:
        steps = jnp.exp(jax.random.uniform(jax.random.fold_in(own, dim), (blocks,), jnp.float32, low / len(split), high / len(split)))
        gain = gain * jnp.repeat(steps, dims[dim] // blocks).reshape([-1 if axis == dim else 1 for axis in range(len(dims))])
    return gain


def noise(key, dims, deviation, bound, shards=(), kind=jnp.bfloat16):
    array = deviation * jax.random.normal(key, dims, jnp.float32)
    if shards:
        array = array * steps_of(key, dims, shards, -0.22, 0.18)
    return jnp.clip(array, -bound, bound).astype(kind)


def setup_inputs(seed: int = 0) -> dict:
    key_list = jax.random.split(jax.random.key(seed), 8)
    facets = noise(key_list[0], (FACETS, 2, SUB, FACET_LEN), 1.0, 6.0, ((0, 4), (2, 8)), jnp.float32)
    facet_offsets = with_ends(jax.random.randint(key_list[1], (FACETS,), 0, N_IMG), jax.random.fold_in(key_list[1], 1), 0, N_IMG - 1).astype(jnp.int32)
    grid_offsets = with_ends(jax.random.randint(key_list[2], (SUBGRIDS,), 0, N_IMG), jax.random.fold_in(key_list[2], 1), 0, N_IMG - 1).astype(jnp.int32)
    taper = jnp.clip(jnp.exp(jax.random.uniform(key_list[3], (SUB,), jnp.float32, math.log(0.3), math.log(3.0))), 0.3, 3.0)
    kernels = noise(key_list[4], (KERNELS, 2, SUB), 0.3, 4.0, (), jnp.float32)
    kernel_index = with_ends(jax.random.randint(key_list[5], (SUBGRIDS, SUB), 0, KERNELS), jax.random.fold_in(key_list[5], 1), 0, KERNELS - 1).astype(jnp.int32)
    residual = noise(key_list[6], (SUBGRIDS, 2, SUB, SUB), 1.0, 6.0, ((0, 4), (2, 8)), jnp.float32)
    return dict(facets=facets, facet_offsets=facet_offsets, grid_offsets=grid_offsets, taper=taper, kernels=kernels, kernel_index=kernel_index, residual=residual)


def mod_product(left, right):
    low_part = right % 256
    high_part = right // 256
    return (left * low_part + ((left * high_part) % 256) * 256) % 65536


def window_start(grid_offset):
    return (grid_offset * FACET_LEN) // N_IMG


def phase_all(facet_offsets, grid_offset):
    position = (grid_offset + jnp.arange(SUB, dtype=jnp.int32)) % N_IMG
    product = mod_product(facet_offsets[:, None], position[None, :])
    angle = product.astype(jnp.float32) * (2.0 * math.pi / N_IMG)
    return jnp.cos(angle), jnp.sin(angle)


def reference(facets, facet_offsets, grid_offsets, taper, kernels, kernel_index, residual):
    extended = jnp.concatenate([facets, facets[..., :SUB]], axis=3)

    def step(buffer, inputs):
        grid_offset, indices, resid = inputs
        begin = window_start(grid_offset).astype(jnp.int32)
        window = lax.dynamic_slice_in_dim(extended, begin, SUB, 3)
        phase_real, phase_imag = phase_all(facet_offsets, grid_offset)
        factor_real = (phase_real * taper)[:, None, :]
        factor_imag = (phase_imag * taper)[:, None, :]
        contrib_real = window[:, 0] * factor_real - window[:, 1] * factor_imag
        contrib_imag = window[:, 0] * factor_imag + window[:, 1] * factor_real
        summed = lax.complex(jnp.sum(contrib_real, 0), jnp.sum(contrib_imag, 0))
        grid = jnp.fft.fft(summed, axis=1, norm="ortho")
        spectrum = jnp.fft.fft(grid, axis=0, norm="ortho").T
        chosen = kernels[indices]
        kernel_complex = lax.complex(chosen[:, 0], chosen[:, 1])
        resid_complex = lax.complex(resid[0], resid[1])
        corrected = resid_complex - kernel_complex * spectrum
        back = jnp.fft.ifft(corrected, axis=1, norm="ortho")
        back = jnp.fft.ifft(back.T, axis=1, norm="ortho")
        back_real = jnp.real(back)[None]
        back_imag = jnp.imag(back)[None]
        value_real = (back_real * phase_real[:, None, :] + back_imag * phase_imag[:, None, :]) * taper
        value_imag = (back_imag * phase_real[:, None, :] - back_real * phase_imag[:, None, :]) * taper
        value = jnp.stack([value_real, value_imag], axis=1)
        current = lax.dynamic_slice_in_dim(buffer, begin, SUB, 3)
        return lax.dynamic_update_slice_in_dim(buffer, current + value, begin, 3), None

    initial = jnp.zeros(extended.shape, jnp.float32)
    buffer, _ = lax.scan(step, initial, (grid_offsets, kernel_index, residual))
    return buffer[..., :FACET_LEN].at[..., :SUB].add(buffer[..., FACET_LEN:])
```

```python
import functools
import math

import jax
import jax.numpy as jnp
import numpy as np
from jax import lax
from jax.experimental import pallas as pl
from jax.experimental.pallas import tpu as pltpu
from jax.sharding import PartitionSpec as P

N_IMG = 65536
FACET_LEN = 5120
LANES = 128


def mod_product(left, right):
    low_part = right % 256
    high_part = right // 256
    return (left * low_part + left * high_part % 256 * 256) % N_IMG


def window_start(grid_offset):
    return grid_offset * FACET_LEN // N_IMG


def phase_pair(facet_offset, grid_offset, length):
    position = (grid_offset + jnp.arange(length, dtype=jnp.int32)) % N_IMG
    angle = mod_product(facet_offset, position).astype(jnp.float32) * (2.0 * math.pi / N_IMG)
    return (jnp.cos(angle), jnp.sin(angle))


def split_table(length):
    index = np.arange(length)
    angle = (index[:, None] * index[None, :] % length) * (2.0 * np.pi / length)
    table = np.concatenate([np.cos(angle), np.sin(angle)], axis=1) / math.sqrt(length)
    high = table.astype(jnp.bfloat16)
    low = (table - high.astype(np.float64)).astype(jnp.bfloat16)
    return np.stack([high, low])


def product(values, high_table, low_table):
    high = values.astype(jnp.bfloat16)
    low = (values - high.astype(jnp.float32)).astype(jnp.bfloat16)

    def dot(left, right):
        return jnp.dot(left, right, preferred_element_type=jnp.float32)

    return dot(high, high_table) + (dot(low, high_table) + dot(high, low_table))


def rotate(values, high_table, low_table, sign):
    rows = values.shape[0] // 2
    both = product(values, high_table, low_table)
    length = both.shape[1] // 2
    real = both[:rows, :length] - sign * both[rows:, length:]
    imag = both[rows:, :length] + sign * both[:rows, length:]
    return real, imag


def lane_block(index):
    return pl.ds(pl.multiple_of(index * LANES, LANES), LANES)


def window_kernel(count, blocks, offsets, ids, columns, factor, *refs):
    outs, (buffer, sems) = refs[:-2], refs[-2:]
    total = columns.shape[3] // LANES

    def begin_of(item):
        return lax.div(offsets[ids[item]] * FACET_LEN, N_IMG)

    def copy(item, piece):
        source = lax.rem(lax.div(begin_of(item), LANES) + piece, total)
        return pltpu.make_async_copy(
            columns.at[0, :, :, lane_block(source)],
            buffer.at[item, :, :, pl.ds(piece * LANES, LANES)],
            sems.at[item, piece],
        )

    for item in range(count):
        for piece in range(blocks + 1):
            copy(item, piece).start()
    lane = lax.broadcasted_iota(jnp.int32, (columns.shape[2], LANES), 1)
    for item in range(count):
        for piece in range(blocks + 1):
            copy(item, piece).wait()
        shift = lax.rem(begin_of(item), LANES)
        back = lax.rem(LANES - shift, LANES)
        keep = lane < LANES - shift
        for piece in range(blocks):
            span = pl.ds(piece * LANES, LANES)
            after = pl.ds((piece + 1) * LANES, LANES)
            parts = []
            for part in range(2):
                first = pltpu.roll(buffer[item, part, :, span], back, 1)
                second = pltpu.roll(buffer[item, part, :, after], back, 1)
                parts.append(jnp.where(keep, first, second))
            real, imag = parts
            factor_real = factor[ids[item], 0:1, span]
            factor_imag = factor[ids[item], 1:2, span]
            outs[item][0, :, span] = real * factor_real - imag * factor_imag
            outs[item][1, :, span] = real * factor_imag + imag * factor_real


def split_out(values, chip, outs):
    for distance, out in enumerate(outs):
        out[...] = values[:, :, lane_block(jnp.bitwise_xor(chip, distance))]


def first_kernel(place, table, *refs):
    chips = place_count(refs)
    terms, outs, scratch = refs[: -1 - chips], refs[-1 - chips : -1], refs[-1]
    total = terms[0][...]
    for term in terms[1:]:
        total = total + term[...]
    rows, length = total.shape[1:]
    real, imag = rotate(total.reshape(2 * rows, length), table[0], table[1], -1.0)
    scratch[0] = real
    scratch[1] = imag
    split_out(scratch, place[0], outs)


def place_count(refs):
    scratch = refs[-1]
    return scratch.shape[2] // LANES


def cross_kernel(sign, place, table, *refs):
    blocks, (keep, send, gathered, partial) = refs[:-4], refs[-4:]
    chip, core = place[0], place[1]
    rows = blocks[0].shape[1]
    for distance, block in enumerate(blocks):
        spot = pl.ds(pl.multiple_of(jnp.bitwise_xor(chip, distance) * rows, rows), rows)
        gathered[0, spot, :] = block[0]
        gathered[1, spot, :] = block[1]
    values = jnp.concatenate([gathered[0].T, gathered[1].T], axis=0)

    def own(half):
        pieces = [
            table[half, pl.ds(pl.multiple_of((2 * index + core) * rows, rows), rows), :]
            for index in range(len(blocks))
        ]
        return jnp.concatenate(pieces, axis=0)

    real, imag = rotate(values, own(0), own(1), sign)
    partial[0] = real
    partial[1] = imag
    mine = pl.ds(pl.multiple_of(core * rows, rows), rows)
    other = pl.ds(pl.multiple_of((1 - core) * rows, rows), rows)
    keep[...] = partial[:, mine, :]
    send[...] = partial[:, other, :]


def correct_kernel(place, table, keep, received, residual, chosen, *refs):
    outs, scratch = refs[:-1], refs[-1]
    rows, length = keep.shape[1:]
    spectrum_real = keep[0] + received[0]
    spectrum_imag = keep[1] + received[1]
    real = residual[0] - (chosen[0] * spectrum_real - chosen[1] * spectrum_imag)
    imag = residual[1] - (chosen[0] * spectrum_imag + chosen[1] * spectrum_real)
    values = jnp.concatenate([real, imag], axis=0)
    real, imag = rotate(values, table[0], table[1], 1.0)
    scratch[0] = real
    scratch[1] = imag
    split_out(scratch, place[0], outs)


def update_kernel(count, blocks, offsets, ids, factor, *refs):
    pairs, out = refs[:-1], refs[-1]
    total = out.shape[3] // LANES
    out[...] = jnp.zeros(out.shape, jnp.float32)
    lane = lax.broadcasted_iota(jnp.int32, (out.shape[2], LANES), 1)
    for item in range(count):
        real_ref, imag_ref = pairs[2 * item], pairs[2 * item + 1]
        begin = lax.div(offsets[ids[item]] * FACET_LEN, N_IMG)
        shift = lax.rem(begin, LANES)
        block = lax.div(begin, LANES)
        late = lane >= shift
        earlier = [jnp.zeros(lane.shape, jnp.float32)] * 2
        for piece in range(blocks + 1):
            if piece < blocks:
                span = pl.ds(piece * LANES, LANES)
                real, imag = real_ref[:, span], imag_ref[:, span]
                factor_real = factor[ids[item], 0:1, span]
                factor_imag = factor[ids[item], 1:2, span]
                turned = [
                    pltpu.roll(real * factor_real + imag * factor_imag, shift, 1),
                    pltpu.roll(imag * factor_real - real * factor_imag, shift, 1),
                ]
            else:
                turned = [jnp.zeros(lane.shape, jnp.float32)] * 2
            spot = lane_block(lax.rem(block + piece, total))
            for part in range(2):
                out[0, part, :, spot] += jnp.where(late, turned[part], earlier[part])
            earlier = turned


VMEM = pl.BlockSpec(memory_space=pltpu.VMEM)
SMEM = pl.BlockSpec(memory_space=pltpu.SMEM)
ANY = pl.BlockSpec(memory_space=pl.ANY)


def call(kernel, outs, scratch, specs, limit, name, cost):
    return pl.pallas_call(
        kernel,
        out_shape=[jax.ShapeDtypeStruct(shape, jnp.float32) for shape in outs],
        in_specs=specs,
        out_specs=[VMEM] * len(outs),
        scratch_shapes=scratch,
        compiler_params=pltpu.CompilerParams(vmem_limit_bytes=limit),
        cost_estimate=pl.CostEstimate(flops=cost, bytes_accessed=cost // 64, transcendentals=0),
        name=name,
    )


def grid_of(count):
    slow = max(step for step in range(1, math.isqrt(count) + 1) if count % step == 0)
    return slow, count // slow


def tiled_device(
    facet_count, team_count, facets, facet_offsets, grid_offsets, taper, kernels, kernel_index, residual
):
    rows = facets.shape[2]
    length = taper.shape[0]
    facet_len = facets.shape[3]
    blocks = length // LANES
    chips = team_count // 2
    per_facet = residual.shape[0]
    slow, fast = grid_of(facet_count)
    facet = lax.axis_index("facet")
    team = lax.axis_index("team")
    place = jnp.stack([team // 2, team % 2]).astype(jnp.int32)
    table = jnp.asarray(split_table(length))
    taper_row = taper[None, :]
    phase_real, phase_imag = jax.vmap(
        lambda offset: phase_pair(facet_offsets[facet], offset, length)
    )(grid_offsets)
    factor = jnp.stack([phase_real * taper_row, phase_imag * taper_row], axis=1)

    def near(step_slow, step_fast):
        down, right = facet // fast, facet % fast
        return (down + step_slow) % slow * fast + (right + step_fast) % fast

    def move(value, step_slow, step_fast):
        pairs = [
            (
                spot,
                (spot // fast + step_slow) % slow * fast + (spot % fast + step_fast) % fast,
            )
            for spot in range(facet_count)
        ]
        return lax.ppermute(value, "facet", pairs)

    def jump(value, distance):
        pairs = [
            (spot, (spot // 2 ^ distance) * 2 + spot % 2) for spot in range(team_count)
        ]
        return lax.ppermute(value, "team", pairs)

    def swap(value):
        return lax.ppermute(value, "team", [(spot, spot ^ 1) for spot in range(team_count)])

    steps = [(i, j) for i in range(slow) for j in range(fast)]
    slow_steps, fast_steps = range(1, slow), range(1, fast)
    onehot = (kernel_index[:, :, None] == jnp.arange(kernels.shape[0], dtype=jnp.int32)).astype(
        jnp.float32
    )
    chosen = jnp.einsum("srk,kac->sarc", onehot, kernels, precision=lax.Precision.HIGHEST)
    block_shape = (2, rows, length)
    piece_shape = (2, rows, LANES)
    mib = 1 << 20
    matmul_cost = 2 * (2 * rows) * length * (2 * length) * 3

    def windows(chunk):
        ids = jnp.stack([near(*step) * per_facet + chunk for step in steps]).astype(jnp.int32)
        outs = call(
            functools.partial(window_kernel, facet_count, blocks),
            [block_shape] * facet_count,
            [
                pltpu.VMEM((facet_count, 2, rows, length + LANES), jnp.float32),
                pltpu.SemaphoreType.DMA((facet_count, blocks + 1)),
            ],
            [SMEM, SMEM, ANY, VMEM],
            8 * mib,
            f"window_{chunk}",
            matmul_cost // 4,
        )(grid_offsets, ids, facets, factor)
        return dict(zip(steps, outs))

    def scatter_first(terms):
        by_fast = {
            (i, j): move(terms[i, j][0], 0, j) for i in slow_steps for j in fast_steps
        }
        by_slow = {
            (i, j): move(terms[i, j][1], i, 0) for i in slow_steps for j in fast_steps
        }
        return by_fast, by_slow

    def scatter_second(terms, firsts):
        by_fast, by_slow = firsts
        received = [terms[0, 0]]
        for j in fast_steps:
            imag = terms[0, j][1]
            for i in slow_steps:
                imag = imag + by_slow[i, j]
            received.append(move(jnp.stack([terms[0, j][0], imag]), 0, j))
        for i in slow_steps:
            real = terms[i, 0][0]
            for j in fast_steps:
                real = real + by_fast[i, j]
            received.append(move(jnp.stack([real, terms[i, 0][1]]), i, 0))
        return received

    def first_transform(received, chunk):
        return call(
            first_kernel,
            [piece_shape] * chips,
            [pltpu.VMEM(block_shape, jnp.float32)],
            [SMEM, VMEM] + [VMEM] * len(received),
            8 * mib,
            f"first_{chunk}",
            matmul_cost,
        )(place, table, *received)

    def exchange(pieces):
        return [pieces[0]] + [jump(pieces[d], d) for d in range(1, chips)]

    def cross(pieces, sign, name):
        return call(
            functools.partial(cross_kernel, sign),
            [block_shape] * 2,
            [
                pltpu.VMEM((2, chips * rows, LANES), jnp.float32),
                pltpu.VMEM((2, LANES, length), jnp.float32),
            ],
            [SMEM, VMEM] + [VMEM] * chips,
            8 * mib,
            name,
            matmul_cost,
        )(place, table, *pieces)

    def correct(keep, received, chunk):
        return call(
            correct_kernel,
            [piece_shape] * chips,
            [pltpu.VMEM(block_shape, jnp.float32)],
            [SMEM] + [VMEM] * 5,
            8 * mib,
            f"correct_{chunk}",
            matmul_cost,
        )(place, table, keep, received, residual[chunk], chosen[chunk])

    def gather_first(own):
        return (
            {j: move(own, 0, j) for j in fast_steps},
            {i: move(own, i, 0) for i in slow_steps},
        )

    def gather_second(firsts):
        by_fast, by_slow = firsts
        reals = {(i, j): move(by_fast[j][0], i, 0) for i in slow_steps for j in fast_steps}
        imags = {(i, j): move(by_slow[i][1], 0, j) for i in slow_steps for j in fast_steps}
        return reals, imags

    chunks = range(per_facet)
    terms = [windows(chunk) for chunk in chunks]
    firsts = [scatter_first(terms[chunk]) for chunk in chunks]
    received = [scatter_second(terms[chunk], firsts[chunk]) for chunk in chunks]
    pieces = [exchange(first_transform(received[chunk], chunk)) for chunk in chunks]
    halves = [cross(pieces[chunk], -1.0, f"cross_{chunk}") for chunk in chunks]
    swapped = [swap(halves[chunk][1]) for chunk in chunks]
    pieces = [exchange(correct(halves[chunk][0], swapped[chunk], chunk)) for chunk in chunks]
    halves = [cross(pieces[chunk], 1.0, f"restore_{chunk}") for chunk in chunks]
    owns = [halves[chunk][0] + swap(halves[chunk][1]) for chunk in chunks]
    gathers = [gather_first(owns[chunk]) for chunk in chunks]
    corners = [gather_second(gathers[chunk]) for chunk in chunks]

    ids, pairs = [], []
    for chunk in chunks:
        by_fast, by_slow = gathers[chunk]
        reals, imags = corners[chunk]
        for i, j in steps:
            ids.append(near(-i, -j) * per_facet + chunk)
            if i and j:
                pairs += [reals[i, j], imags[i, j]]
            else:
                whole = by_slow[i] if i else by_fast[j] if j else owns[chunk]
                pairs += [whole[0], whole[1]]
    (update,) = call(
        functools.partial(update_kernel, len(ids), blocks),
        [(1, 2, rows, facet_len)],
        [],
        [SMEM, SMEM, VMEM] + [VMEM] * len(pairs),
        16 * mib,
        "update",
        matmul_cost,
    )(grid_offsets, jnp.stack(ids).astype(jnp.int32), factor, *pairs)
    return update


def dft_tables(length):
    index = jnp.arange(length, dtype=jnp.int32)
    angle = (index[:, None] * index[None, :] % length).astype(jnp.float32) * (
        2.0 * math.pi / length
    )
    norm_scale = 1.0 / math.sqrt(length)
    return (jnp.cos(angle) * norm_scale, jnp.sin(angle) * norm_scale)


def transform_last(values, tables, sign):
    cosine, sine = tables
    real_part = values[:, 0]
    imag_part = values[:, 1]

    def multiply(left, right):
        return jnp.einsum("nab,bc->nac", left, right, precision=lax.Precision.HIGHEST)

    out_real = multiply(real_part, cosine) - sign * multiply(imag_part, sine)
    out_imag = multiply(imag_part, cosine) + sign * multiply(real_part, sine)
    return jnp.stack([out_real, out_imag], axis=1)


def plain_device(facets, facet_offsets, grid_offsets, taper, kernels, kernel_index, residual):
    columns = facets[0]
    length = taper.shape[0]
    facet_len = columns.shape[2]
    extended = jnp.concatenate([columns, columns[:, :, :length]], axis=2)
    facet_offset = facet_offsets[lax.axis_index("facet")]
    tables = dft_tables(length)

    def single(grid_offset):
        window = lax.dynamic_slice_in_dim(extended, window_start(grid_offset), length, 2)
        phase_real, phase_imag = phase_pair(facet_offset, grid_offset, length)
        factor_real = phase_real * taper
        factor_imag = phase_imag * taper
        return jnp.stack(
            [
                window[0] * factor_real - window[1] * factor_imag,
                window[0] * factor_imag + window[1] * factor_real,
            ]
        )

    terms = jax.vmap(single)(grid_offsets)
    summed = lax.psum_scatter(terms, "facet", scatter_dimension=0, tiled=True)
    summed = transform_last(summed, tables, -1.0)
    by_rows = lax.all_to_all(summed, "team", split_axis=3, concat_axis=2, tiled=True)
    by_rows = jnp.transpose(by_rows, (0, 1, 3, 2))
    spectrum = transform_last(by_rows, tables, -1.0)
    onehot = (kernel_index[:, :, None] == jnp.arange(kernels.shape[0], dtype=jnp.int32)).astype(
        jnp.float32
    )
    chosen = jnp.einsum("srk,kac->sarc", onehot, kernels, precision=lax.Precision.HIGHEST)
    corr_real = residual[:, 0] - (chosen[:, 0] * spectrum[:, 0] - chosen[:, 1] * spectrum[:, 1])
    corr_imag = residual[:, 1] - (chosen[:, 0] * spectrum[:, 1] + chosen[:, 1] * spectrum[:, 0])
    restored = transform_last(jnp.stack([corr_real, corr_imag], axis=1), tables, 1.0)
    restored = jnp.transpose(restored, (0, 1, 3, 2))
    by_columns = lax.all_to_all(restored, "team", split_axis=2, concat_axis=3, tiled=True)
    by_columns = transform_last(by_columns, tables, 1.0)
    initial = jnp.zeros(extended.shape, jnp.float32)
    piece = lax.all_gather(by_columns, "facet", axis=0, tiled=True)

    def add_one(item, total):
        grid_offset = grid_offsets[item]
        block = lax.dynamic_index_in_dim(piece, item, 0, keepdims=False)
        phase_real, phase_imag = phase_pair(facet_offset, grid_offset, length)
        value = jnp.stack(
            [
                (block[0] * phase_real + block[1] * phase_imag) * taper,
                (block[1] * phase_real - block[0] * phase_imag) * taper,
            ]
        )
        begin = window_start(grid_offset)
        current = lax.dynamic_slice_in_dim(total, begin, length, 2)
        return lax.dynamic_update_slice_in_dim(total, current + value, begin, 2)

    buffer = lax.fori_loop(0, piece.shape[0], add_one, initial)
    update = buffer[:, :, :facet_len].at[:, :, :length].add(buffer[:, :, facet_len:])
    return update[None]


def solution(mesh):
    facet_count, team_count = mesh.shape["facet"], mesh.shape["team"]

    def per_device(*arrays):
        rows, length, facet_len = arrays[0].shape[2], arrays[3].shape[0], arrays[0].shape[3]
        chips = team_count // 2
        tiled = (
            team_count % 2 == 0
            and chips & (chips - 1) == 0
            and 2 * rows == LANES
            and length == chips * LANES
            and facet_len % LANES == 0
            and arrays[6].shape[2] == rows
        )
        if tiled:
            return tiled_device(facet_count, team_count, *arrays)
        return plain_device(*arrays)

    return jax.shard_map(
        per_device,
        mesh=mesh,
        in_specs=(
            P("facet", None, "team", None),
            P(),
            P(),
            P(),
            P(),
            P("facet", "team"),
            P("facet", None, "team", None),
        ),
        out_specs=P("facet", None, "team", None),
        check_vma=False,
    )
```

```python
import functools
import math

import jax
import jax.numpy as jnp
import numpy as np
from jax import lax
from jax.experimental import pallas as pl
from jax.experimental.pallas import tpu as pltpu
from jax.sharding import PartitionSpec as P


N_IMG = 65536
FACET_LEN = 5120
LANES = 128


def mod_product(left, right):
    low_part = right % 256
    high_part = right // 256
    return (left * low_part + left * high_part % 256 * 256) % N_IMG


def window_start(grid_offset):
    return grid_offset * FACET_LEN // N_IMG


def phase_pair(facet_offset, grid_offset, length):
    position = (grid_offset + jnp.arange(length, dtype=jnp.int32)) % N_IMG
    angle = mod_product(facet_offset, position).astype(jnp.float32) * (2.0 * math.pi / N_IMG)
    return (jnp.cos(angle), jnp.sin(angle))


def split_table(length):
    index = np.arange(length)
    angle = (index[:, None] * index[None, :] % length) * (2.0 * np.pi / length)
    table = np.concatenate([np.cos(angle), np.sin(angle)], axis=1) / math.sqrt(length)
    high = table.astype(jnp.bfloat16)
    low = (table - high.astype(np.float64)).astype(jnp.bfloat16)
    return np.stack([high, low])


def product(values, high_table, low_table):
    high = values.astype(jnp.bfloat16)
    low = (values - high.astype(jnp.float32)).astype(jnp.bfloat16)

    def dot(left, right):
        return jnp.dot(left, right, preferred_element_type=jnp.float32)

    return dot(high, high_table) + (dot(low, high_table) + dot(high, low_table))


def rotate(values, high_table, low_table, sign):
    rows = values.shape[0] // 2
    both = product(values, high_table, low_table)
    length = both.shape[1] // 2
    real = both[:rows, :length] - sign * both[rows:, length:]
    imag = both[rows:, :length] + sign * both[:rows, length:]
    return real, imag


def lane_block(index):
    return pl.ds(pl.multiple_of(index * LANES, LANES), LANES)


def begin_of(offset):
    return lax.div(offset * FACET_LEN, N_IMG)


def phase_factor(offsets, facet_offset, taper, factor):
    count, _, length = factor.shape
    row = lax.broadcasted_iota(jnp.int32, (count, length), 0)
    position = lax.broadcasted_iota(jnp.int32, (count, length), 1)
    for item in range(count):
        position = position + jnp.where(row == item, offsets[item], 0)
    position = lax.bitwise_and(position, N_IMG - 1)
    low_part = lax.bitwise_and(position, 255)
    high_part = lax.shift_right_logical(position, 8)
    high_product = lax.bitwise_and(facet_offset * high_part, 255) * 256
    product = lax.bitwise_and(facet_offset * low_part + high_product, N_IMG - 1)
    angle = product.astype(jnp.float32) * (2.0 * math.pi / N_IMG)
    real = jnp.cos(angle) * taper
    imag = jnp.sin(angle) * taper
    for item in range(count):
        factor[item, 0:1, :] = real[item : item + 1, :]
        factor[item, 1:2, :] = imag[item : item + 1, :]


def cut_windows(offsets, ids, columns, outs, buffer, sems, prepare, factor):
    count = len(outs)
    total = columns.shape[3] // LANES
    blocks = factor.shape[2] // LANES

    def copy(item, piece):
        source = lax.rem(lax.div(begin_of(offsets[ids[item]]), LANES) + piece, total)
        return pltpu.make_async_copy(
            columns.at[0, :, :, lane_block(source)],
            buffer.at[item, :, :, pl.ds(piece * LANES, LANES)],
            sems.at[item, piece],
        )

    for item in range(count):
        for piece in range(blocks + 1):
            copy(item, piece).start()
    prepare()
    lane = lax.broadcasted_iota(jnp.int32, (columns.shape[2], LANES), 1)
    for item in range(count):
        for piece in range(blocks + 1):
            copy(item, piece).wait()
        shift = lax.rem(begin_of(offsets[ids[item]]), LANES)
        back = lax.rem(LANES - shift, LANES)
        keep = lane < LANES - shift
        for piece in range(blocks):
            span = pl.ds(piece * LANES, LANES)
            after = pl.ds((piece + 1) * LANES, LANES)
            parts = []
            for part in range(2):
                first = pltpu.roll(buffer[item, part, :, span], back, 1)
                second = pltpu.roll(buffer[item, part, :, after], back, 1)
                parts.append(jnp.where(keep, first, second))
            real, imag = parts
            factor_real = factor[ids[item], 0:1, span]
            factor_imag = factor[ids[item], 1:2, span]
            outs[item][0][:, span] = real * factor_real - imag * factor_imag
            outs[item][1][:, span] = real * factor_imag + imag * factor_real


def corner_window_kernel(
    per_facet, ids, offsets_hbm, facet_offsets_hbm, taper_hbm, columns, *refs
):
    factor, planes = refs[0], refs[1:-6]
    buffer, sems, offsets, facet_offsets, taper, small_sems = refs[-6:]
    small = [
        pltpu.make_async_copy(offsets_hbm, offsets, small_sems.at[0]),
        pltpu.make_async_copy(facet_offsets_hbm, facet_offsets, small_sems.at[1]),
        pltpu.make_async_copy(taper_hbm, taper, small_sems.at[2]),
    ]
    for copy in small:
        copy.start()
    small[0].wait()
    outs = [
        (planes[2 * step].at[chunk], planes[2 * step + 1].at[chunk])
        for step in range(len(planes) // 2)
        for chunk in range(per_facet)
    ]

    def prepare():
        small[1].wait()
        small[2].wait()
        phase_factor(offsets, facet_offsets[ids[len(outs)]], taper[...], factor)

    cut_windows(offsets, ids, columns, outs, buffer, sems, prepare, factor)


def window_kernel(offsets, ids, columns, factor, *refs):
    planes, (buffer, sems) = refs[:-2], refs[-2:]
    outs = [(plane.at[0], plane.at[1]) for plane in planes]
    cut_windows(offsets, ids, columns, outs, buffer, sems, lambda: None, factor)


def join_kernel(part, chunk, term, *refs):
    received, out = refs[:-1], refs[-1]
    total = term[part]
    for corner in received:
        total = total + corner[chunk]
    out[part] = total
    out[1 - part] = term[1 - part]


def split_out(values, chip, outs):
    for distance, out in enumerate(outs):
        out[...] = values[:, :, lane_block(jnp.bitwise_xor(chip, distance))]


def first_kernel(place, table, *refs):
    scratch = refs[-1]
    chips = scratch.shape[2] // LANES
    terms, outs = refs[: -1 - chips], refs[-1 - chips : -1]
    total = terms[0][...]
    for term in terms[1:]:
        total = total + term[...]
    rows, length = total.shape[1:]
    real, imag = rotate(total.reshape(2 * rows, length), table[0], table[1], -1.0)
    scratch[0] = real
    scratch[1] = imag
    split_out(scratch, place[0], outs)


def cross_kernel(sign, place, table, *refs):
    blocks, (keep, send, gathered, partial) = refs[:-4], refs[-4:]
    chip, core = place[0], place[1]
    rows = blocks[0].shape[1]
    for distance, block in enumerate(blocks):
        spot = pl.ds(pl.multiple_of(jnp.bitwise_xor(chip, distance) * rows, rows), rows)
        gathered[0, spot, :] = block[0]
        gathered[1, spot, :] = block[1]
    values = jnp.concatenate([gathered[0].T, gathered[1].T], axis=0)

    def own(half):
        pieces = [
            table[half, pl.ds(pl.multiple_of((2 * index + core) * rows, rows), rows), :]
            for index in range(len(blocks))
        ]
        return jnp.concatenate(pieces, axis=0)

    real, imag = rotate(values, own(0), own(1), sign)
    partial[0] = real
    partial[1] = imag
    mine = pl.ds(pl.multiple_of(core * rows, rows), rows)
    other = pl.ds(pl.multiple_of((1 - core) * rows, rows), rows)
    keep[...] = partial[:, mine, :]
    send[...] = partial[:, other, :]


def correct_kernel(place, table, keep, received, residual, chosen, *refs):
    outs, scratch = refs[:-1], refs[-1]
    spectrum_real = keep[0] + received[0]
    spectrum_imag = keep[1] + received[1]
    real = residual[0] - (chosen[0] * spectrum_real - chosen[1] * spectrum_imag)
    imag = residual[1] - (chosen[0] * spectrum_imag + chosen[1] * spectrum_real)
    values = jnp.concatenate([real, imag], axis=0)
    real, imag = rotate(values, table[0], table[1], 1.0)
    scratch[0] = real
    scratch[1] = imag
    split_out(scratch, place[0], outs)


def turned_pieces(offset, factor, real_ref, imag_ref):
    rows, length = real_ref.shape
    blocks = length // LANES
    begin = begin_of(offset)
    shift = lax.rem(begin, LANES)
    lane = lax.broadcasted_iota(jnp.int32, (rows, LANES), 1)
    late = lane >= shift
    empty = jnp.zeros((rows, LANES), jnp.float32)
    earlier = [empty, empty]
    pieces = []
    for piece in range(blocks + 1):
        turned = [empty, empty]
        if piece < blocks:
            span = pl.ds(piece * LANES, LANES)
            real, imag = real_ref[:, span], imag_ref[:, span]
            factor_real, factor_imag = factor[0:1, span], factor[1:2, span]
            turned = [
                pltpu.roll(real * factor_real + imag * factor_imag, shift, 1),
                pltpu.roll(imag * factor_real - real * factor_imag, shift, 1),
            ]
        pieces.append([jnp.where(late, turned[part], earlier[part]) for part in range(2)])
        earlier = turned
    return lax.div(begin, LANES), pieces


def update_kernel(layout, offsets, ids, factor, *refs):
    arrays, (out, window) = list(refs[:-2]), refs[-2:]
    pairs = []
    for planes in layout:
        if planes == 1:
            whole = arrays.pop(0)
            pairs.append((whole.at[0], whole.at[1]))
        else:
            pairs.append((arrays.pop(0), arrays.pop(0)))
    count = len(pairs)
    total = out.shape[3] // LANES
    out[...] = jnp.zeros(out.shape, jnp.float32)
    for item in range(count):
        block, pieces = turned_pieces(
            offsets[ids[item]], factor.at[ids[item]], *pairs[item]
        )
        for piece, parts in enumerate(pieces):
            spot = lane_block(lax.rem(block + piece, total))
            for part in range(2):
                out[0, part, :, spot] += parts[part]
    block = lax.div(begin_of(offsets[ids[count]]), LANES)
    for piece in range(window.shape[2] // LANES):
        spot = lane_block(lax.rem(block + piece, total))
        window[:, :, pl.ds(piece * LANES, LANES)] = out[0, :, :, spot]


def finish_kernel(offsets, ids, factor, window, real, imag, whole, out, buffer, sems):
    total = out.shape[3] // LANES
    item = ids[0]
    block, pieces = turned_pieces(offsets[item], factor.at[item], real, imag)

    def copy(piece):
        return pltpu.make_async_copy(
            buffer.at[piece],
            out.at[0, :, :, lane_block(lax.rem(block + piece, total))],
            sems.at[piece],
        )

    for piece, parts in enumerate(pieces):
        span = pl.ds(piece * LANES, LANES)
        for part in range(2):
            buffer[piece, part] = window[part, :, span] + parts[part]
        copy(piece).start()
    for piece in range(len(pieces)):
        copy(piece).wait()


VMEM = pl.BlockSpec(memory_space=pltpu.VMEM)
SMEM = pl.BlockSpec(memory_space=pltpu.SMEM)
HBM = pl.BlockSpec(memory_space=pltpu.HBM)
MIB = 1 << 20


def call(kernel, outs, scratch, specs, limit, cost, **kwargs):
    return pl.pallas_call(
        kernel,
        out_shape=[jax.ShapeDtypeStruct(shape, jnp.float32) for shape in outs],
        in_specs=specs,
        out_specs=kwargs.pop("out_specs", [VMEM] * len(outs)),
        scratch_shapes=scratch,
        compiler_params=pltpu.CompilerParams(vmem_limit_bytes=limit),
        cost_estimate=pl.CostEstimate(flops=cost, bytes_accessed=cost // 64, transcendentals=0),
        **kwargs,
    )


def grid_of(count):
    slow = max(step for step in range(1, math.isqrt(count) + 1) if count % step == 0)
    return slow, count // slow


def tiled_device(
    facet_count, team_count, facets, facet_offsets, grid_offsets, taper, kernels, kernel_index, residual
):
    rows = facets.shape[2]
    length = taper.shape[0]
    facet_len = facets.shape[3]
    blocks = length // LANES
    chips = team_count // 2
    per_facet = residual.shape[0]
    subgrids = grid_offsets.shape[0]
    slow, fast = grid_of(facet_count)
    facet = lax.axis_index("facet")
    team = lax.axis_index("team")
    place = jnp.stack([team // 2, team % 2]).astype(jnp.int32)
    table = jnp.asarray(split_table(length))
    down, right = facet // fast, facet % fast

    def near(step, chunk):
        to = (down + step[0]) % slow * fast + (right + step[1]) % fast
        return to * per_facet + chunk

    def listed(values):
        return jnp.stack(values).astype(jnp.int32)

    def move(value, step_slow, step_fast):
        pairs = [
            (
                spot,
                (spot // fast + step_slow) % slow * fast + (spot % fast + step_fast) % fast,
            )
            for spot in range(facet_count)
        ]
        return lax.ppermute(value, "facet", pairs)

    def exchange(pieces):
        out = [pieces[0]]
        for distance in range(1, chips):
            pairs = [
                (spot, (spot // 2 ^ distance) * 2 + spot % 2) for spot in range(team_count)
            ]
            out.append(lax.ppermute(pieces[distance], "team", pairs))
        return out

    def swap(value):
        return lax.ppermute(value, "team", [(spot, spot ^ 1) for spot in range(team_count)])

    slow_steps, fast_steps = range(1, slow), range(1, fast)
    near_steps = [(0, j) for j in fast_steps] + [(i, 0) for i in slow_steps]
    corner_steps = [(i, j) for i in slow_steps for j in fast_steps]
    onehot = (kernel_index[:, :, None] == jnp.arange(kernels.shape[0], dtype=jnp.int32)).astype(
        jnp.float32
    )
    chosen = jnp.einsum("srk,kac->sarc", onehot, kernels, precision=lax.Precision.HIGHEST)
    block_shape = (2, rows, length)
    piece_shape = (2, rows, LANES)
    matmul_cost = 2 * (2 * rows) * length * (2 * length) * 3
    chunks = range(per_facet)

    def window_scratch(count):
        return [
            pltpu.VMEM((count, 2, rows, length + LANES), jnp.float32),
            pltpu.SemaphoreType.DMA((count, blocks + 1)),
        ]

    def in_hbm(value):
        return pltpu.with_memory_space_constraint(value, pltpu.HBM)

    columns = in_hbm(facets)
    corner_keys = [(step, chunk) for step in corner_steps for chunk in chunks]
    factor, *planes = call(
        functools.partial(corner_window_kernel, per_facet),
        [(subgrids, 2, length)] + [(per_facet, rows, length)] * (2 * len(corner_steps)),
        window_scratch(len(corner_keys))
        + [
            pltpu.SMEM(grid_offsets.shape, jnp.int32),
            pltpu.SMEM(facet_offsets.shape, jnp.int32),
            pltpu.VMEM((1, length), jnp.float32),
            pltpu.SemaphoreType.DMA((3,)),
        ],
        [SMEM, HBM, HBM, HBM, HBM],
        8 * MIB,
        matmul_cost // 8,
    )(
        listed([near(step, chunk) for step, chunk in corner_keys] + [facet]),
        in_hbm(grid_offsets),
        in_hbm(facet_offsets),
        in_hbm(taper.reshape(1, length)),
        columns,
    )
    by_fast, by_slow = {}, {}
    for spot, (i, j) in enumerate(corner_steps):
        by_fast[i, j] = move(planes[2 * spot], 0, j)
        by_slow[i, j] = move(planes[2 * spot + 1], i, 0)

    near_keys = [(step, chunk) for chunk in chunks for step in [(0, 0)] + near_steps]
    outs = call(
        window_kernel,
        [block_shape] * len(near_keys),
        window_scratch(len(near_keys)),
        [SMEM, SMEM, HBM, VMEM],
        12 * MIB,
        matmul_cost // 4,
    )(grid_offsets, listed([near(step, chunk) for step, chunk in near_keys]), columns, factor)
    terms = dict(zip(near_keys, outs))

    def join(term, corners, part, chunk):
        if not corners:
            return term
        (joined,) = call(
            functools.partial(join_kernel, part, chunk),
            [block_shape],
            [],
            [VMEM] * (1 + len(corners)),
            2 * MIB,
            matmul_cost // 64,
        )(term, *corners)
        return joined

    def scatter(chunk):
        received = [terms[(0, 0), chunk]]
        for i in slow_steps:
            corners = [by_fast[i, j] for j in fast_steps]
            joined = join(terms[(i, 0), chunk], corners, 0, chunk)
            received.append(move(joined, i, 0))
        for j in fast_steps:
            corners = [by_slow[i, j] for i in slow_steps]
            joined = join(terms[(0, j), chunk], corners, 1, chunk)
            received.append(move(joined, 0, j))
        return received

    def first_transform(received):
        return call(
            first_kernel,
            [piece_shape] * chips,
            [pltpu.VMEM(block_shape, jnp.float32)],
            [SMEM, VMEM] + [VMEM] * len(received),
            8 * MIB,
            matmul_cost,
        )(place, table, *received)

    def cross(pieces, sign):
        return call(
            functools.partial(cross_kernel, sign),
            [block_shape] * 2,
            [
                pltpu.VMEM((2, chips * rows, LANES), jnp.float32),
                pltpu.VMEM((2, LANES, length), jnp.float32),
            ],
            [SMEM, VMEM] + [VMEM] * chips,
            8 * MIB,
            matmul_cost,
        )(place, table, *pieces)

    def correct(keep, received, chunk):
        return call(
            correct_kernel,
            [piece_shape] * chips,
            [pltpu.VMEM(block_shape, jnp.float32)],
            [SMEM] + [VMEM] * 5,
            8 * MIB,
            matmul_cost,
        )(place, table, keep, received, residual[chunk], chosen[chunk])

    def gather(own):
        found = {(0, 0): (own,)}
        for j in fast_steps:
            found[0, j] = (move(own, 0, j),)
        for i in slow_steps:
            found[i, 0] = (move(own, i, 0),)
        for i, j in corner_steps:
            found[i, j] = (move(found[0, j][0][0], i, 0), move(found[i, 0][0][1], 0, j))
        return found

    received = [scatter(chunk) for chunk in chunks]
    pieces = [exchange(first_transform(received[chunk])) for chunk in chunks]
    halves = [cross(pieces[chunk], -1.0) for chunk in chunks]
    swapped = [swap(halves[chunk][1]) for chunk in chunks]
    pieces = [exchange(correct(halves[chunk][0], swapped[chunk], chunk)) for chunk in chunks]
    halves = [cross(pieces[chunk], 1.0) for chunk in chunks]
    ids, items = [], []
    for chunk in chunks:
        keep, sent = halves[chunk]
        own = keep + swap(sent)
        for (i, j), found in gather(own).items():
            ids.append(near((-i, -j), chunk))
            items.append(found)
    ids = listed(ids)
    *first_items, last_item = items
    if len(last_item) == 1:
        last_item = (last_item[0][0], last_item[0][1])
    arrays = [array for item in first_items for array in item]
    whole, window = call(
        functools.partial(update_kernel, tuple(len(item) for item in first_items)),
        [(1, 2, rows, facet_len), (2, rows, length + LANES)],
        [],
        [SMEM, SMEM, VMEM] + [VMEM] * len(arrays),
        16 * MIB,
        matmul_cost,
    )(grid_offsets, ids, factor, *arrays)
    (update,) = call(
        finish_kernel,
        [(1, 2, rows, facet_len)],
        [
            pltpu.VMEM((blocks + 1, 2, rows, LANES), jnp.float32),
            pltpu.SemaphoreType.DMA((blocks + 1,)),
        ],
        [SMEM, SMEM, VMEM, VMEM, VMEM, VMEM, HBM],
        8 * MIB,
        matmul_cost // 8,
        out_specs=[HBM],
        input_output_aliases={6: 0},
    )(grid_offsets, ids[-1:], factor, window, *last_item, whole)
    return update


def dft_tables(length):
    index = jnp.arange(length, dtype=jnp.int32)
    angle = (index[:, None] * index[None, :] % length).astype(jnp.float32) * (
        2.0 * math.pi / length
    )
    norm_scale = 1.0 / math.sqrt(length)
    return (jnp.cos(angle) * norm_scale, jnp.sin(angle) * norm_scale)


def transform_last(values, tables, sign):
    cosine, sine = tables
    real_part = values[:, 0]
    imag_part = values[:, 1]

    def multiply(left, right):
        return jnp.einsum("nab,bc->nac", left, right, precision=lax.Precision.HIGHEST)

    out_real = multiply(real_part, cosine) - sign * multiply(imag_part, sine)
    out_imag = multiply(imag_part, cosine) + sign * multiply(real_part, sine)
    return jnp.stack([out_real, out_imag], axis=1)


def plain_device(facets, facet_offsets, grid_offsets, taper, kernels, kernel_index, residual):
    columns = facets[0]
    length = taper.shape[0]
    facet_len = columns.shape[2]
    extended = jnp.concatenate([columns, columns[:, :, :length]], axis=2)
    facet_offset = facet_offsets[lax.axis_index("facet")]
    tables = dft_tables(length)

    def single(grid_offset):
        window = lax.dynamic_slice_in_dim(extended, window_start(grid_offset), length, 2)
        phase_real, phase_imag = phase_pair(facet_offset, grid_offset, length)
        factor_real = phase_real * taper
        factor_imag = phase_imag * taper
        return jnp.stack(
            [
                window[0] * factor_real - window[1] * factor_imag,
                window[0] * factor_imag + window[1] * factor_real,
            ]
        )

    terms = jax.vmap(single)(grid_offsets)
    summed = lax.psum_scatter(terms, "facet", scatter_dimension=0, tiled=True)
    summed = transform_last(summed, tables, -1.0)
    by_rows = lax.all_to_all(summed, "team", split_axis=3, concat_axis=2, tiled=True)
    by_rows = jnp.transpose(by_rows, (0, 1, 3, 2))
    spectrum = transform_last(by_rows, tables, -1.0)
    onehot = (kernel_index[:, :, None] == jnp.arange(kernels.shape[0], dtype=jnp.int32)).astype(
        jnp.float32
    )
    chosen = jnp.einsum("srk,kac->sarc", onehot, kernels, precision=lax.Precision.HIGHEST)
    corr_real = residual[:, 0] - (chosen[:, 0] * spectrum[:, 0] - chosen[:, 1] * spectrum[:, 1])
    corr_imag = residual[:, 1] - (chosen[:, 0] * spectrum[:, 1] + chosen[:, 1] * spectrum[:, 0])
    restored = transform_last(jnp.stack([corr_real, corr_imag], axis=1), tables, 1.0)
    restored = jnp.transpose(restored, (0, 1, 3, 2))
    by_columns = lax.all_to_all(restored, "team", split_axis=2, concat_axis=3, tiled=True)
    by_columns = transform_last(by_columns, tables, 1.0)
    initial = jnp.zeros(extended.shape, jnp.float32)
    piece = lax.all_gather(by_columns, "facet", axis=0, tiled=True)

    def add_one(item, total):
        grid_offset = grid_offsets[item]
        block = lax.dynamic_index_in_dim(piece, item, 0, keepdims=False)
        phase_real, phase_imag = phase_pair(facet_offset, grid_offset, length)
        value = jnp.stack(
            [
                (block[0] * phase_real + block[1] * phase_imag) * taper,
                (block[1] * phase_real - block[0] * phase_imag) * taper,
            ]
        )
        begin = window_start(grid_offset)
        current = lax.dynamic_slice_in_dim(total, begin, length, 2)
        return lax.dynamic_update_slice_in_dim(total, current + value, begin, 2)

    buffer = lax.fori_loop(0, piece.shape[0], add_one, initial)
    update = buffer[:, :, :facet_len].at[:, :, :length].add(buffer[:, :, facet_len:])
    return update[None]


def solution(mesh):
    facet_count, team_count = mesh.shape["facet"], mesh.shape["team"]

    def per_device(*arrays):
        rows, length, facet_len = arrays[0].shape[2], arrays[3].shape[0], arrays[0].shape[3]
        chips = team_count // 2
        tiled = (
            team_count % 2 == 0
            and chips & (chips - 1) == 0
            and 2 * rows == LANES
            and length == chips * LANES
            and facet_len % LANES == 0
            and arrays[6].shape[2] == rows
        )
        if tiled:
            return tiled_device(facet_count, team_count, *arrays)
        return plain_device(*arrays)

    return jax.shard_map(
        per_device,
        mesh=mesh,
        in_specs=(
            P("facet", None, "team", None),
            P(),
            P(),
            P(),
            P(),
            P("facet", "team"),
            P("facet", None, "team", None),
        ),
        out_specs=P("facet", None, "team", None),
        check_vma=False,
    )
```

```python
import functools
import math

import jax
import jax.numpy as jnp
import numpy as np
from jax import lax
from jax.experimental import pallas as pl
from jax.experimental.pallas import tpu as pltpu
from jax.sharding import PartitionSpec as P


N_IMG = 65536
FACET_LEN = 5120
LANES = 128
CHIP, CORE, FACET = range(3)


def mod_product(left, right):
    low_part = right % 256
    high_part = right // 256
    return (left * low_part + left * high_part % 256 * 256) % N_IMG


def window_start(grid_offset):
    return grid_offset * FACET_LEN // N_IMG


def phase_pair(facet_offset, grid_offset, length):
    position = (grid_offset + jnp.arange(length, dtype=jnp.int32)) % N_IMG
    angle = mod_product(facet_offset, position).astype(jnp.float32) * (2.0 * math.pi / N_IMG)
    return (jnp.cos(angle), jnp.sin(angle))


def split_table(length):
    index = np.arange(length)
    angle = (index[:, None] * index[None, :] % length) * (2.0 * np.pi / length)
    table = np.concatenate([np.cos(angle), np.sin(angle)], axis=1) / math.sqrt(length)
    high = table.astype(jnp.bfloat16)
    low = (table - high.astype(np.float64)).astype(jnp.bfloat16)
    return np.stack([high, low])


def product(values, high_table, low_table):
    high = values.astype(jnp.bfloat16)
    low = (values - high.astype(jnp.float32)).astype(jnp.bfloat16)

    def dot(left, right):
        return jnp.dot(left, right, preferred_element_type=jnp.float32)

    return dot(high, high_table) + (dot(low, high_table) + dot(high, low_table))


def rotate(values, high_table, low_table, sign):
    rows = values.shape[0] // 2
    both = product(values, high_table, low_table)
    length = both.shape[1] // 2
    real = both[:rows, :length] - sign * both[rows:, length:]
    imag = both[rows:, :length] + sign * both[:rows, length:]
    return real, imag


def lane_block(index):
    return pl.ds(pl.multiple_of(index * LANES, LANES), LANES)


def begin_of(offset):
    return lax.div(offset * FACET_LEN, N_IMG)


def phase_factor(offsets, facet_offset, taper, factor):
    count, _, length = factor.shape
    row = lax.broadcasted_iota(jnp.int32, (count, length), 0)
    position = lax.broadcasted_iota(jnp.int32, (count, length), 1)
    for item in range(count):
        position = position + jnp.where(row == item, offsets[item], 0)
    position = lax.bitwise_and(position, N_IMG - 1)
    low_part = lax.bitwise_and(position, 255)
    high_part = lax.shift_right_logical(position, 8)
    high_product = lax.bitwise_and(facet_offset * high_part, 255) * 256
    product = lax.bitwise_and(facet_offset * low_part + high_product, N_IMG - 1)
    angle = product.astype(jnp.float32) * (2.0 * math.pi / N_IMG)
    real = jnp.cos(angle) * taper
    imag = jnp.sin(angle) * taper
    for item in range(count):
        factor[item, 0:1, :] = real[item : item + 1, :]
        factor[item, 1:2, :] = imag[item : item + 1, :]


def pairs_of(layout, refs):
    refs = list(refs)
    pairs = []
    for planes in layout:
        if planes == 1:
            whole = refs.pop(0)
            pairs.append((whole.at[0], whole.at[1]))
        else:
            pairs.append((refs.pop(0), refs.pop(0)))
    return pairs


def cut_windows(offsets, ids, columns, outs, buffer, sems, prepare, factor):
    count = len(outs)
    total = columns.shape[3] // LANES
    blocks = factor.shape[2] // LANES

    def copy(item, piece):
        source = lax.rem(lax.div(begin_of(offsets[ids[item]]), LANES) + piece, total)
        return pltpu.make_async_copy(
            columns.at[0, :, :, lane_block(source)],
            buffer.at[item, :, :, pl.ds(piece * LANES, LANES)],
            sems.at[item, piece],
        )

    for item in range(count):
        for piece in range(blocks + 1):
            copy(item, piece).start()
    prepare()
    lane = lax.broadcasted_iota(jnp.int32, (columns.shape[2], LANES), 1)
    for item in range(count):
        for piece in range(blocks + 1):
            copy(item, piece).wait()
        shift = lax.rem(begin_of(offsets[ids[item]]), LANES)
        back = lax.rem(LANES - shift, LANES)
        keep = lane < LANES - shift
        for piece in range(blocks):
            span = pl.ds(piece * LANES, LANES)
            after = pl.ds((piece + 1) * LANES, LANES)
            parts = []
            for part in range(2):
                first = pltpu.roll(buffer[item, part, :, span], back, 1)
                second = pltpu.roll(buffer[item, part, :, after], back, 1)
                parts.append(jnp.where(keep, first, second))
            real, imag = parts
            factor_real = factor[ids[item], 0:1, span]
            factor_imag = factor[ids[item], 1:2, span]
            outs[item][0][:, span] = real * factor_real - imag * factor_imag
            outs[item][1][:, span] = real * factor_imag + imag * factor_real


def corner_window_kernel(
    per_facet, spots, info, offsets_hbm, facet_offsets_hbm, taper_hbm, columns, *refs
):
    factor, planes = refs[0], refs[1:-6]
    buffer, sems, offsets, facet_offsets, taper, small_sems = refs[-6:]
    small = [
        pltpu.make_async_copy(offsets_hbm, offsets, small_sems.at[0]),
        pltpu.make_async_copy(facet_offsets_hbm, facet_offsets, small_sems.at[1]),
        pltpu.make_async_copy(taper_hbm, taper, small_sems.at[2]),
    ]
    for copy in small:
        copy.start()
    small[0].wait()
    outs = [
        (planes[2 * step].at[chunk], planes[2 * step + 1].at[chunk])
        for step in range(len(planes) // 2)
        for chunk in range(per_facet)
    ]

    def prepare():
        small[1].wait()
        small[2].wait()
        phase_factor(offsets, facet_offsets[info[FACET]], taper[...], factor)

    ids = [info[spot] for spot in spots]
    cut_windows(offsets, ids, columns, outs, buffer, sems, prepare, factor)


def window_kernel(layout, spots, info, offsets, columns, factor, *refs):
    planes, (buffer, sems) = refs[:-2], refs[-2:]
    outs = pairs_of(layout, planes)
    ids = [info[spot] for spot in spots]
    cut_windows(offsets, ids, columns, outs, buffer, sems, lambda: None, factor)


def join_kernel(part, chunk, whole, term, *refs):
    received, out = refs[:-1], refs[-1]
    if not whole:
        total = term[...]
    else:
        total = term[part]
        out[1 - part] = term[1 - part]
    for corner in received:
        total = total + corner[chunk]
    if whole:
        out[part] = total
    else:
        out[...] = total


def choose_kernel(index, kernels, out):
    chunks, _, rows, _ = out.shape
    for chunk in range(chunks):

        def step(row, carry):
            found = kernels[index[chunk, row]]
            out[chunk, 0, pl.ds(row, 1), :] = found[0:1]
            out[chunk, 1, pl.ds(row, 1), :] = found[1:2]
            return carry

        lax.fori_loop(0, rows, step, 0, unroll=8)


def split_out(values, chip, outs):
    for distance, out in enumerate(outs):
        out[...] = values[:, :, lane_block(jnp.bitwise_xor(chip, distance))]


def first_kernel(layout, info, table, *refs):
    scratch = refs[-1]
    chips = scratch.shape[2] // LANES
    terms, outs = refs[: -1 - chips], refs[-1 - chips : -1]
    pairs = pairs_of(layout, terms)
    sums = []
    for part in range(2):
        total = pairs[0][part][...]
        for pair in pairs[1:]:
            total = total + pair[part][...]
        sums.append(total)
    real, imag = rotate(jnp.concatenate(sums, axis=0), table[0], table[1], -1.0)
    scratch[0] = real
    scratch[1] = imag
    split_out(scratch, info[CHIP], outs)


def cross_kernel(sign, info, table, *refs):
    blocks, (keep, send, gathered, partial) = refs[:-4], refs[-4:]
    chip, core = info[CHIP], info[CORE]
    rows = blocks[0].shape[1]
    for distance, block in enumerate(blocks):
        spot = pl.ds(pl.multiple_of(jnp.bitwise_xor(chip, distance) * rows, rows), rows)
        gathered[0, spot, :] = block[0]
        gathered[1, spot, :] = block[1]
    values = jnp.concatenate([gathered[0].T, gathered[1].T], axis=0)

    def own(half):
        pieces = [
            table[half, pl.ds(pl.multiple_of((2 * index + core) * rows, rows), rows), :]
            for index in range(len(blocks))
        ]
        return jnp.concatenate(pieces, axis=0)

    real, imag = rotate(values, own(0), own(1), sign)
    partial[0] = real
    partial[1] = imag
    mine = pl.ds(pl.multiple_of(core * rows, rows), rows)
    other = pl.ds(pl.multiple_of((1 - core) * rows, rows), rows)
    keep[...] = partial[:, mine, :]
    send[...] = partial[:, other, :]


def correct_kernel(chunk, info, table, keep, received, residuals, chosens, *refs):
    outs, scratch = refs[:-1], refs[-1]
    residual, chosen = residuals.at[chunk], chosens.at[chunk]
    spectrum_real = keep[0] + received[0]
    spectrum_imag = keep[1] + received[1]
    real = residual[0] - (chosen[0] * spectrum_real - chosen[1] * spectrum_imag)
    imag = residual[1] - (chosen[0] * spectrum_imag + chosen[1] * spectrum_real)
    values = jnp.concatenate([real, imag], axis=0)
    real, imag = rotate(values, table[0], table[1], 1.0)
    scratch[0] = real
    scratch[1] = imag
    split_out(scratch, info[CHIP], outs)


def turned_pieces(offset, factor, real_ref, imag_ref):
    rows, length = real_ref.shape
    blocks = length // LANES
    begin = begin_of(offset)
    shift = lax.rem(begin, LANES)
    lane = lax.broadcasted_iota(jnp.int32, (rows, LANES), 1)
    late = lane >= shift
    empty = jnp.zeros((rows, LANES), jnp.float32)
    earlier = [empty, empty]
    pieces = []
    for piece in range(blocks + 1):
        turned = [empty, empty]
        if piece < blocks:
            span = pl.ds(piece * LANES, LANES)
            real, imag = real_ref[:, span], imag_ref[:, span]
            factor_real, factor_imag = factor[0:1, span], factor[1:2, span]
            turned = [
                pltpu.roll(real * factor_real + imag * factor_imag, shift, 1),
                pltpu.roll(imag * factor_real - real * factor_imag, shift, 1),
            ]
        pieces.append([jnp.where(late, turned[part], earlier[part]) for part in range(2)])
        earlier = turned
    return lax.div(begin, LANES), pieces


def update_kernel(layout, spots, info, offsets, factor, *refs):
    arrays, (out, window) = refs[:-2], refs[-2:]
    pairs = pairs_of(layout, arrays)
    ids = [info[spot] for spot in spots]
    count = len(pairs)
    total = out.shape[3] // LANES
    out[...] = jnp.zeros(out.shape, jnp.float32)
    for item in range(count):
        block, pieces = turned_pieces(
            offsets[ids[item]], factor.at[ids[item]], *pairs[item]
        )
        for piece, parts in enumerate(pieces):
            spot = lane_block(lax.rem(block + piece, total))
            for part in range(2):
                out[0, part, :, spot] += parts[part]
    block = lax.div(begin_of(offsets[ids[count]]), LANES)
    for piece in range(window.shape[2] // LANES):
        spot = lane_block(lax.rem(block + piece, total))
        window[:, :, pl.ds(piece * LANES, LANES)] = out[0, :, :, spot]


def finish_kernel(spot, info, offsets, factor, window, real, imag, whole, out, buffer, sems):
    total = out.shape[3] // LANES
    item = info[spot]
    block, pieces = turned_pieces(offsets[item], factor.at[item], real, imag)

    def copy(piece):
        return pltpu.make_async_copy(
            buffer.at[piece],
            out.at[0, :, :, lane_block(lax.rem(block + piece, total))],
            sems.at[piece],
        )

    for piece, parts in enumerate(pieces):
        span = pl.ds(piece * LANES, LANES)
        for part in range(2):
            buffer[piece, part] = window[part, :, span] + parts[part]
        copy(piece).start()
    for piece in range(len(pieces)):
        copy(piece).wait()


VMEM = pl.BlockSpec(memory_space=pltpu.VMEM)
SMEM = pl.BlockSpec(memory_space=pltpu.SMEM)
HBM = pl.BlockSpec(memory_space=pltpu.HBM)
MIB = 1 << 20


def call(kernel, outs, scratch, specs, limit, cost, **kwargs):
    return pl.pallas_call(
        kernel,
        out_shape=[jax.ShapeDtypeStruct(shape, jnp.float32) for shape in outs],
        in_specs=specs,
        out_specs=kwargs.pop("out_specs", [VMEM] * len(outs)),
        scratch_shapes=scratch,
        compiler_params=pltpu.CompilerParams(vmem_limit_bytes=limit),
        cost_estimate=pl.CostEstimate(flops=cost, bytes_accessed=cost // 64, transcendentals=0),
        **kwargs,
    )


def jump_order(chips):
    return list(range(chips - 1, 0, -1))


def grid_of(count):
    slow = max(step for step in range(1, math.isqrt(count) + 1) if count % step == 0)
    return slow, count // slow


def tiled_device(
    facet_count, team_count, facets, facet_offsets, grid_offsets, taper, kernels, kernel_index, residual
):
    rows = facets.shape[2]
    length = taper.shape[0]
    facet_len = facets.shape[3]
    blocks = length // LANES
    chips = team_count // 2
    per_facet = residual.shape[0]
    subgrids = grid_offsets.shape[0]
    slow, fast = grid_of(facet_count)
    facet = lax.axis_index("facet")
    team = lax.axis_index("team")
    table = jnp.asarray(split_table(length))
    down, right = facet // fast, facet % fast

    def near(step, chunk):
        to = (down + step[0]) % slow * fast + (right + step[1]) % fast
        return to * per_facet + chunk

    def move(value, step_slow, step_fast):
        pairs = [
            (
                spot,
                (spot // fast + step_slow) % slow * fast + (spot % fast + step_fast) % fast,
            )
            for spot in range(facet_count)
        ]
        return lax.ppermute(value, "facet", pairs)

    def exchange(pieces):
        out = [pieces[0]] + [None] * (chips - 1)
        for distance in jump_order(chips):
            pairs = [
                (spot, (spot // 2 ^ distance) * 2 + spot % 2) for spot in range(team_count)
            ]
            out[distance] = lax.ppermute(pieces[distance], "team", pairs)
        return out

    def swap(value):
        return lax.ppermute(value, "team", [(spot, spot ^ 1) for spot in range(team_count)])

    slow_steps, fast_steps = range(1, slow), range(1, fast)
    near_steps = [(0, j) for j in fast_steps] + [(i, 0) for i in slow_steps]
    corner_steps = [(i, j) for i in slow_steps for j in fast_steps]
    plane = (rows, length)
    block_shape = (2, rows, length)
    piece_shape = (2, rows, LANES)
    matmul_cost = 2 * (2 * rows) * length * (2 * length) * 3
    chunks = range(per_facet)

    def window_scratch(count):
        return [
            pltpu.VMEM((count, 2, rows, length + LANES), jnp.float32),
            pltpu.SemaphoreType.DMA((count, blocks + 1)),
        ]

    last = per_facet - 1
    corner_keys = [(step, chunk) for step in corner_steps for chunk in chunks]
    near_keys = [(step, chunk) for chunk in chunks for step in [(0, 0)] + near_steps]
    gather_keys = [
        ((-i, -j), chunk) for chunk in chunks for i, j in [(0, 0)] + near_steps + corner_steps
    ]
    spots, numbers = {}, [team // 2, team % 2, facet]
    for key in corner_keys + near_keys + gather_keys:
        spots[key] = len(numbers)
        numbers.append(near(*key))
    info = jnp.stack(numbers).astype(jnp.int32)

    def in_hbm(value):
        return pltpu.with_memory_space_constraint(value, pltpu.HBM)

    columns = in_hbm(facets)
    factor, *planes = call(
        functools.partial(corner_window_kernel, per_facet, [spots[key] for key in corner_keys]),
        [(subgrids, 2, length)] + [(per_facet, rows, length)] * (2 * len(corner_steps)),
        window_scratch(len(corner_keys))
        + [
            pltpu.SMEM(grid_offsets.shape, jnp.int32),
            pltpu.SMEM(facet_offsets.shape, jnp.int32),
            pltpu.VMEM((1, length), jnp.float32),
            pltpu.SemaphoreType.DMA((3,)),
        ],
        [SMEM, HBM, HBM, HBM, HBM],
        8 * MIB,
        matmul_cost // 8,
    )(
        info,
        in_hbm(grid_offsets),
        in_hbm(facet_offsets),
        in_hbm(taper.reshape(1, length)),
        columns,
    )
    by_fast, by_slow = {}, {}
    for spot, (i, j) in enumerate(corner_steps):
        by_fast[i, j] = move(planes[2 * spot], 0, j)
        by_slow[i, j] = move(planes[2 * spot + 1], i, 0)

    near_layout = [2 if chunk == 0 and step != (0, 0) else 1 for step, chunk in near_keys]
    outs = call(
        functools.partial(window_kernel, near_layout, [spots[key] for key in near_keys]),
        [shape for count in near_layout for shape in ([block_shape], [plane] * 2)[count - 1]],
        window_scratch(len(near_keys)),
        [SMEM, SMEM, HBM, VMEM],
        12 * MIB,
        matmul_cost // 4,
    )(info, grid_offsets, columns, factor)
    terms = {}
    for key, count in zip(near_keys, near_layout):
        terms[key], outs = tuple(outs[:count]), outs[count:]

    (chosen,) = call(
        choose_kernel, [residual.shape], [], [SMEM, VMEM], 4 * MIB, matmul_cost // 8
    )(kernel_index, kernels)

    def join(term, corners, part, chunk):
        if not corners:
            return term
        (joined,) = call(
            functools.partial(join_kernel, part, chunk, term.ndim == 3),
            [term.shape],
            [],
            [VMEM] * (1 + len(corners)),
            2 * MIB,
            matmul_cost // 64,
        )(term, *corners)
        return joined

    def scatter(chunk):
        received = [terms[(0, 0), chunk]]
        for i, j in near_steps:
            axis = "slow" if i else "fast"
            part = 0 if i else 1
            if i:
                corners = [by_fast[i, j] for j in fast_steps]
            else:
                corners = [by_slow[i, j] for i in slow_steps]
            i, j = (i, 0) if axis == "slow" else (0, j)
            term = terms[(i, j), chunk]
            if len(term) == 1:
                joined = join(term[0], corners, part, chunk)
                received.append((move(joined, i, j),))
            else:
                early = move(term[1 - part], i, j)
                joined = join(term[part], corners, part, chunk)
                late = move(joined, i, j)
                received.append((late, early) if part == 0 else (early, late))
        return received

    def first_transform(received):
        arrays = [array for item in received for array in item]
        return call(
            functools.partial(first_kernel, [len(item) for item in received]),
            [piece_shape] * chips,
            [pltpu.VMEM(block_shape, jnp.float32)],
            [SMEM, VMEM] + [VMEM] * len(arrays),
            8 * MIB,
            matmul_cost,
        )(info, table, *arrays)

    def cross(pieces, sign):
        return call(
            functools.partial(cross_kernel, sign),
            [block_shape] * 2,
            [
                pltpu.VMEM((2, chips * rows, LANES), jnp.float32),
                pltpu.VMEM((2, LANES, length), jnp.float32),
            ],
            [SMEM, VMEM] + [VMEM] * chips,
            8 * MIB,
            matmul_cost,
        )(info, table, *pieces)

    def correct(keep, received, chunk):
        return call(
            functools.partial(correct_kernel, chunk),
            [piece_shape] * chips,
            [pltpu.VMEM(block_shape, jnp.float32)],
            [SMEM] + [VMEM] * 5,
            8 * MIB,
            matmul_cost,
        )(info, table, keep, received, residual, chosen)

    def gather(own, chunk):
        found = {(0, 0): (own,)}
        split = chunk == last
        for i, j in near_steps:
            if split:
                part = 1 if i else 0
                early = move(own[part], i, j)
                late = move(own[1 - part], i, j)
                found[i, j] = (late, early) if part else (early, late)
            else:
                whole = move(own, i, j)
                found[i, j] = (whole,)

        def part_of(item, part):
            return item[part] if len(item) == 2 else item[0][part]

        for i, j in corner_steps:
            found[i, j] = (move(part_of(found[0, j], 0), i, 0), move(part_of(found[i, 0], 1), 0, j))
        return found

    received = [scatter(chunk) for chunk in chunks]
    pieces = [exchange(first_transform(received[chunk])) for chunk in chunks]
    halves = [cross(pieces[chunk], -1.0) for chunk in chunks]
    swapped = [swap(halves[chunk][1]) for chunk in chunks]
    pieces = [exchange(correct(halves[chunk][0], swapped[chunk], chunk)) for chunk in chunks]
    halves = [cross(pieces[chunk], 1.0) for chunk in chunks]
    keys, items = [], []
    for chunk in chunks:
        keep, sent = halves[chunk]
        own = keep + swap(sent)
        for (i, j), found in gather(own, chunk).items():
            keys.append(spots[(-i, -j), chunk])
            items.append(found)
    *first_items, last_item = items
    if len(last_item) == 1:
        last_item = (last_item[0][0], last_item[0][1])
    arrays = [array for item in first_items for array in item]
    whole, window = call(
        functools.partial(update_kernel, [len(item) for item in first_items], keys),
        [(1, 2, rows, facet_len), (2, rows, length + LANES)],
        [],
        [SMEM, SMEM, VMEM] + [VMEM] * len(arrays),
        16 * MIB,
        matmul_cost,
    )(info, grid_offsets, factor, *arrays)
    (update,) = call(
        functools.partial(finish_kernel, keys[-1]),
        [(1, 2, rows, facet_len)],
        [
            pltpu.VMEM((blocks + 1, 2, rows, LANES), jnp.float32),
            pltpu.SemaphoreType.DMA((blocks + 1,)),
        ],
        [SMEM, SMEM, VMEM, VMEM, VMEM, VMEM, HBM],
        8 * MIB,
        matmul_cost // 8,
        out_specs=[HBM],
        input_output_aliases={6: 0},
    )(info, grid_offsets, factor, window, *last_item, whole)
    return update


def dft_tables(length):
    index = jnp.arange(length, dtype=jnp.int32)
    angle = (index[:, None] * index[None, :] % length).astype(jnp.float32) * (
        2.0 * math.pi / length
    )
    norm_scale = 1.0 / math.sqrt(length)
    return (jnp.cos(angle) * norm_scale, jnp.sin(angle) * norm_scale)


def transform_last(values, tables, sign):
    cosine, sine = tables
    real_part = values[:, 0]
    imag_part = values[:, 1]

    def multiply(left, right):
        return jnp.einsum("nab,bc->nac", left, right, precision=lax.Precision.HIGHEST)

    out_real = multiply(real_part, cosine) - sign * multiply(imag_part, sine)
    out_imag = multiply(imag_part, cosine) + sign * multiply(real_part, sine)
    return jnp.stack([out_real, out_imag], axis=1)


def plain_device(facets, facet_offsets, grid_offsets, taper, kernels, kernel_index, residual):
    columns = facets[0]
    length = taper.shape[0]
    facet_len = columns.shape[2]
    extended = jnp.concatenate([columns, columns[:, :, :length]], axis=2)
    facet_offset = facet_offsets[lax.axis_index("facet")]
    tables = dft_tables(length)

    def single(grid_offset):
        window = lax.dynamic_slice_in_dim(extended, window_start(grid_offset), length, 2)
        phase_real, phase_imag = phase_pair(facet_offset, grid_offset, length)
        factor_real = phase_real * taper
        factor_imag = phase_imag * taper
        return jnp.stack(
            [
                window[0] * factor_real - window[1] * factor_imag,
                window[0] * factor_imag + window[1] * factor_real,
            ]
        )

    terms = jax.vmap(single)(grid_offsets)
    summed = lax.psum_scatter(terms, "facet", scatter_dimension=0, tiled=True)
    summed = transform_last(summed, tables, -1.0)
    by_rows = lax.all_to_all(summed, "team", split_axis=3, concat_axis=2, tiled=True)
    by_rows = jnp.transpose(by_rows, (0, 1, 3, 2))
    spectrum = transform_last(by_rows, tables, -1.0)
    onehot = (kernel_index[:, :, None] == jnp.arange(kernels.shape[0], dtype=jnp.int32)).astype(
        jnp.float32
    )
    chosen = jnp.einsum("srk,kac->sarc", onehot, kernels, precision=lax.Precision.HIGHEST)
    corr_real = residual[:, 0] - (chosen[:, 0] * spectrum[:, 0] - chosen[:, 1] * spectrum[:, 1])
    corr_imag = residual[:, 1] - (chosen[:, 0] * spectrum[:, 1] + chosen[:, 1] * spectrum[:, 0])
    restored = transform_last(jnp.stack([corr_real, corr_imag], axis=1), tables, 1.0)
    restored = jnp.transpose(restored, (0, 1, 3, 2))
    by_columns = lax.all_to_all(restored, "team", split_axis=2, concat_axis=3, tiled=True)
    by_columns = transform_last(by_columns, tables, 1.0)
    initial = jnp.zeros(extended.shape, jnp.float32)
    piece = lax.all_gather(by_columns, "facet", axis=0, tiled=True)

    def add_one(item, total):
        grid_offset = grid_offsets[item]
        block = lax.dynamic_index_in_dim(piece, item, 0, keepdims=False)
        phase_real, phase_imag = phase_pair(facet_offset, grid_offset, length)
        value = jnp.stack(
            [
                (block[0] * phase_real + block[1] * phase_imag) * taper,
                (block[1] * phase_real - block[0] * phase_imag) * taper,
            ]
        )
        begin = window_start(grid_offset)
        current = lax.dynamic_slice_in_dim(total, begin, length, 2)
        return lax.dynamic_update_slice_in_dim(total, current + value, begin, 2)

    buffer = lax.fori_loop(0, piece.shape[0], add_one, initial)
    update = buffer[:, :, :facet_len].at[:, :, :length].add(buffer[:, :, facet_len:])
    return update[None]


def solution(mesh):
    facet_count, team_count = mesh.shape["facet"], mesh.shape["team"]

    def per_device(*arrays):
        rows, length, facet_len = arrays[0].shape[2], arrays[3].shape[0], arrays[0].shape[3]
        chips = team_count // 2
        tiled = (
            team_count % 2 == 0
            and chips & (chips - 1) == 0
            and 2 * rows == LANES
            and length == chips * LANES
            and facet_len % LANES == 0
            and arrays[6].shape[2] == rows
        )
        if tiled:
            return tiled_device(facet_count, team_count, *arrays)
        return plain_device(*arrays)

    return jax.shard_map(
        per_device,
        mesh=mesh,
        in_specs=(
            P("facet", None, "team", None),
            P(),
            P(),
            P(),
            P(),
            P("facet", "team"),
            P("facet", None, "team", None),
        ),
        out_specs=P("facet", None, "team", None),
        check_vma=False,
    )
```

```python
import functools
import math

import jax
import jax.numpy as jnp
import numpy as np
from jax import lax
from jax.experimental import pallas as pl
from jax.experimental.pallas import tpu as pltpu
from jax.sharding import PartitionSpec as P


N_IMG = 65536
FACET_LEN = 5120
LANES = 128
SLOW, FAST = range(2)


def mod_product(left, right):
    low_part = right % 256
    high_part = right // 256
    return (left * low_part + left * high_part % 256 * 256) % N_IMG


def window_start(grid_offset):
    return grid_offset * FACET_LEN // N_IMG


def phase_pair(facet_offset, grid_offset, length):
    position = (grid_offset + jnp.arange(length, dtype=jnp.int32)) % N_IMG
    angle = mod_product(facet_offset, position).astype(jnp.float32) * (2.0 * math.pi / N_IMG)
    return (jnp.cos(angle), jnp.sin(angle))


def split_table(length):
    index = np.arange(length)
    angle = (index[:, None] * index[None, :] % length) * (2.0 * np.pi / length)
    table = np.concatenate([np.cos(angle), np.sin(angle)], axis=1) / math.sqrt(length)
    high = table.astype(jnp.bfloat16)
    low = (table - high.astype(np.float64)).astype(jnp.bfloat16)
    return np.stack([high, low])


def product(values, high_table, low_table):
    high = values.astype(jnp.bfloat16)
    low = (values - high.astype(jnp.float32)).astype(jnp.bfloat16)

    def dot(left, right):
        return jnp.dot(left, right, preferred_element_type=jnp.float32)

    rows = values.shape[0]
    both = dot(jnp.concatenate([high, low], axis=0), high_table)
    return both[:rows] + (both[rows:] + dot(high, low_table))


def rotate(values, high_table, low_table, sign):
    rows = values.shape[0] // 2
    both = product(values, high_table, low_table)
    length = both.shape[1] // 2
    real = both[:rows, :length] - sign * both[rows:, length:]
    imag = both[rows:, :length] + sign * both[:rows, length:]
    return real, imag


def chip_and_core():
    team = lax.axis_index("team")
    return lax.div(team, 2), lax.rem(team, 2)


def lane_block(index):
    return pl.ds(pl.multiple_of(index * LANES, LANES), LANES)


def begin_of(offset):
    return lax.div(offset * FACET_LEN, N_IMG)


def phase_factor(offsets, facet_offset, taper, factor):
    count, _, length = factor.shape
    row = lax.broadcasted_iota(jnp.int32, (count, length), 0)
    position = lax.broadcasted_iota(jnp.int32, (count, length), 1)
    for item in range(count):
        position = position + jnp.where(row == item, offsets[item], 0)
    position = lax.bitwise_and(position, N_IMG - 1)
    low_part = lax.bitwise_and(position, 255)
    high_part = lax.shift_right_logical(position, 8)
    high_product = lax.bitwise_and(facet_offset * high_part, 255) * 256
    product = lax.bitwise_and(facet_offset * low_part + high_product, N_IMG - 1)
    angle = product.astype(jnp.float32) * (2.0 * math.pi / N_IMG)
    real = jnp.cos(angle) * taper
    imag = jnp.sin(angle) * taper
    for item in range(count):
        factor[item, 0:1, :] = real[item : item + 1, :]
        factor[item, 1:2, :] = imag[item : item + 1, :]


def pairs_of(layout, refs):
    refs = list(refs)
    pairs = []
    for planes in layout:
        if planes == 1:
            whole = refs.pop(0)
            pairs.append((whole.at[0], whole.at[1]))
        else:
            pairs.append((refs.pop(0), refs.pop(0)))
    return pairs


def cut_windows(offsets, ids, columns, outs, buffer, sems, prepare, factor):
    count = len(outs)
    total = columns.shape[3] // LANES
    blocks = factor.shape[2] // LANES

    def copy(item, piece):
        source = lax.rem(lax.div(begin_of(offsets[ids[item]]), LANES) + piece, total)
        return pltpu.make_async_copy(
            columns.at[0, :, :, lane_block(source)],
            buffer.at[item, :, :, pl.ds(piece * LANES, LANES)],
            sems.at[item, piece],
        )

    for item in range(count):
        for piece in range(blocks + 1):
            copy(item, piece).start()
    prepare()
    lane = lax.broadcasted_iota(jnp.int32, (columns.shape[2], LANES), 1)
    for item in range(count):
        for piece in range(blocks + 1):
            copy(item, piece).wait()
        shift = lax.rem(begin_of(offsets[ids[item]]), LANES)
        back = lax.rem(LANES - shift, LANES)
        keep = lane < LANES - shift
        for piece in range(blocks):
            span = pl.ds(piece * LANES, LANES)
            after = pl.ds((piece + 1) * LANES, LANES)
            parts = []
            for part in range(2):
                first = pltpu.roll(buffer[item, part, :, span], back, 1)
                second = pltpu.roll(buffer[item, part, :, after], back, 1)
                parts.append(jnp.where(keep, first, second))
            real, imag = parts
            factor_real = factor[ids[item], 0:1, span]
            factor_imag = factor[ids[item], 1:2, span]
            outs[item][0][:, span] = real * factor_real - imag * factor_imag
            outs[item][1][:, span] = real * factor_imag + imag * factor_real


def corner_window_kernel(
    per_facet, near, keys, offsets_hbm, facet_offsets_hbm, taper_hbm, columns, *refs
):
    factor, planes = refs[0], refs[1:-6]
    buffer, sems, offsets, facet_offsets, taper, small_sems = refs[-6:]
    small = [
        pltpu.make_async_copy(offsets_hbm, offsets, small_sems.at[0]),
        pltpu.make_async_copy(facet_offsets_hbm, facet_offsets, small_sems.at[1]),
        pltpu.make_async_copy(taper_hbm, taper, small_sems.at[2]),
    ]
    for copy in small:
        copy.start()
    small[0].wait()
    outs = [
        (planes[2 * step].at[chunk], planes[2 * step + 1].at[chunk])
        for step in range(len(planes) // 2)
        for chunk in range(per_facet)
    ]

    def prepare():
        small[1].wait()
        small[2].wait()
        phase_factor(offsets, facet_offsets[lax.axis_index("facet")], taper[...], factor)

    ids = [near(*key) for key in keys]
    cut_windows(offsets, ids, columns, outs, buffer, sems, prepare, factor)


def window_kernel(layout, near, keys, offsets, columns, factor, *refs):
    planes, (buffer, sems) = refs[:-2], refs[-2:]
    outs = pairs_of(layout, planes)
    ids = [near(*key) for key in keys]
    cut_windows(offsets, ids, columns, outs, buffer, sems, lambda: None, factor)


def join_kernel(part, chunk, whole, term, *refs):
    received, out = refs[:-1], refs[-1]
    if not whole:
        total = term[...]
    else:
        total = term[part]
        out[1 - part] = term[1 - part]
    for corner in received:
        total = total + corner[chunk]
    if whole:
        out[part] = total
    else:
        out[...] = total


def choose_kernel(index, kernels, out):
    chunks, _, rows, _ = out.shape
    for chunk in range(chunks):

        def step(row, carry):
            found = kernels[index[chunk, row]]
            out[chunk, 0, pl.ds(row, 1), :] = found[0:1]
            out[chunk, 1, pl.ds(row, 1), :] = found[1:2]
            return carry

        lax.fori_loop(0, rows, step, 0, unroll=8)


def split_out(values, outs):
    chip, _ = chip_and_core()
    for distance, out in enumerate(outs):
        out[...] = values[:, :, lane_block(jnp.bitwise_xor(chip, distance))]


def first_kernel(layout, table, *refs):
    scratch = refs[-1]
    chips = scratch.shape[2] // LANES
    terms, outs = refs[: -1 - chips], refs[-1 - chips : -1]
    pairs = pairs_of(layout, terms)
    sums = []
    for part in range(2):
        total = pairs[0][part][...]
        for pair in pairs[1:]:
            total = total + pair[part][...]
        sums.append(total)
    real, imag = rotate(jnp.concatenate(sums, axis=0), table[0], table[1], -1.0)
    scratch[0] = real
    scratch[1] = imag
    split_out(scratch, outs)


def cross_kernel(sign, table, *refs):
    blocks, (keep, send, gathered, partial) = refs[:-4], refs[-4:]
    chip, core = chip_and_core()
    rows = blocks[0].shape[1]
    for distance, block in enumerate(blocks):
        spot = pl.ds(pl.multiple_of(jnp.bitwise_xor(chip, distance) * rows, rows), rows)
        gathered[0, spot, :] = block[0]
        gathered[1, spot, :] = block[1]
    values = jnp.concatenate([gathered[0].T, gathered[1].T], axis=0)

    def own(half):
        pieces = [
            table[half, pl.ds(pl.multiple_of((2 * index + core) * rows, rows), rows), :]
            for index in range(len(blocks))
        ]
        return jnp.concatenate(pieces, axis=0)

    real, imag = rotate(values, own(0), own(1), sign)
    partial[0] = real
    partial[1] = imag
    mine = pl.ds(pl.multiple_of(core * rows, rows), rows)
    other = pl.ds(pl.multiple_of((1 - core) * rows, rows), rows)
    keep[...] = partial[:, mine, :]
    send[...] = partial[:, other, :]


def correct_kernel(chunk, table, keep, received, residuals, chosens, *refs):
    outs, scratch = refs[:-1], refs[-1]
    residual, chosen = residuals.at[chunk], chosens.at[chunk]
    spectrum_real = keep[0] + received[0]
    spectrum_imag = keep[1] + received[1]
    real = residual[0] - (chosen[0] * spectrum_real - chosen[1] * spectrum_imag)
    imag = residual[1] - (chosen[0] * spectrum_imag + chosen[1] * spectrum_real)
    values = jnp.concatenate([real, imag], axis=0)
    real, imag = rotate(values, table[0], table[1], 1.0)
    scratch[0] = real
    scratch[1] = imag
    split_out(scratch, outs)


def turned_pieces(offset, factor, real_ref, imag_ref):
    rows, length = real_ref.shape
    blocks = length // LANES
    begin = begin_of(offset)
    shift = lax.rem(begin, LANES)
    lane = lax.broadcasted_iota(jnp.int32, (rows, LANES), 1)
    late = lane >= shift
    empty = jnp.zeros((rows, LANES), jnp.float32)
    earlier = [empty, empty]
    pieces = []
    for piece in range(blocks + 1):
        turned = [empty, empty]
        if piece < blocks:
            span = pl.ds(piece * LANES, LANES)
            real, imag = real_ref[:, span], imag_ref[:, span]
            factor_real, factor_imag = factor[0:1, span], factor[1:2, span]
            turned = [
                pltpu.roll(real * factor_real + imag * factor_imag, shift, 1),
                pltpu.roll(imag * factor_real - real * factor_imag, shift, 1),
            ]
        pieces.append([jnp.where(late, turned[part], earlier[part]) for part in range(2)])
        earlier = turned
    return lax.div(begin, LANES), pieces


def update_kernel(layout, near, keys, offsets, factor, *refs):
    arrays, (out, window) = refs[:-2], refs[-2:]
    pairs = pairs_of(layout, arrays)
    ids = [near(*key) for key in keys]
    count = len(pairs)
    total = out.shape[3] // LANES
    out[...] = jnp.zeros(out.shape, jnp.float32)
    for item in range(count):
        block, pieces = turned_pieces(
            offsets[ids[item]], factor.at[ids[item]], *pairs[item]
        )
        for piece, parts in enumerate(pieces):
            spot = lane_block(lax.rem(block + piece, total))
            for part in range(2):
                out[0, part, :, spot] += parts[part]
    block = lax.div(begin_of(offsets[ids[count]]), LANES)
    for piece in range(window.shape[2] // LANES):
        spot = lane_block(lax.rem(block + piece, total))
        window[:, :, pl.ds(piece * LANES, LANES)] = out[0, :, :, spot]


def finish_kernel(near, key, offsets, factor, window, real, imag, whole, out, buffer, sems):
    total = out.shape[3] // LANES
    item = near(*key)
    block, pieces = turned_pieces(offsets[item], factor.at[item], real, imag)

    def copy(piece):
        return pltpu.make_async_copy(
            buffer.at[piece],
            out.at[0, :, :, lane_block(lax.rem(block + piece, total))],
            sems.at[piece],
        )

    for piece, parts in enumerate(pieces):
        span = pl.ds(piece * LANES, LANES)
        for part in range(2):
            buffer[piece, part] = window[part, :, span] + parts[part]
        copy(piece).start()
    for piece in range(len(pieces)):
        copy(piece).wait()


VMEM = pl.BlockSpec(memory_space=pltpu.VMEM)
SMEM = pl.BlockSpec(memory_space=pltpu.SMEM)
HBM = pl.BlockSpec(memory_space=pltpu.HBM)
MIB = 1 << 20


def call(kernel, outs, scratch, specs, limit, cost, **kwargs):
    return pl.pallas_call(
        kernel,
        out_shape=[jax.ShapeDtypeStruct(shape, jnp.float32) for shape in outs],
        in_specs=specs,
        out_specs=kwargs.pop("out_specs", [VMEM] * len(outs)),
        scratch_shapes=scratch,
        compiler_params=pltpu.CompilerParams(vmem_limit_bytes=limit),
        cost_estimate=pl.CostEstimate(flops=cost, bytes_accessed=cost // 64, transcendentals=0),
        **kwargs,
    )


def jump_order(chips):
    return list(range(chips - 1, 0, -1))


def grid_of(count):
    slow = max(step for step in range(1, math.isqrt(count) + 1) if count % step == 0)
    return slow, count // slow


def tiled_device(
    facet_count, team_count, facets, facet_offsets, grid_offsets, taper, kernels, kernel_index, residual
):
    rows = facets.shape[2]
    length = taper.shape[0]
    facet_len = facets.shape[3]
    blocks = length // LANES
    chips = team_count // 2
    per_facet = residual.shape[0]
    subgrids = grid_offsets.shape[0]
    slow, fast = grid_of(facet_count)
    table = jnp.asarray(split_table(length))

    def near(step, chunk):
        facet = lax.axis_index("facet")
        down, right = lax.div(facet, fast), lax.rem(facet, fast)
        to = lax.rem(down + step[0] % slow, slow) * fast + lax.rem(right + step[1] % fast, fast)
        return to * per_facet + chunk

    def move(value, step_slow, step_fast):
        pairs = [
            (
                spot,
                (spot // fast + step_slow) % slow * fast + (spot % fast + step_fast) % fast,
            )
            for spot in range(facet_count)
        ]
        return lax.ppermute(value, "facet", pairs)

    def exchange(pieces):
        out = [pieces[0]] + [None] * (chips - 1)
        for distance in jump_order(chips):
            pairs = [
                (spot, (spot // 2 ^ distance) * 2 + spot % 2) for spot in range(team_count)
            ]
            out[distance] = lax.ppermute(pieces[distance], "team", pairs)
        return out

    def swap(value):
        return lax.ppermute(value, "team", [(spot, spot ^ 1) for spot in range(team_count)])

    slow_steps, fast_steps = range(1, slow), range(1, fast)
    near_steps = [(0, j) for j in fast_steps] + [(i, 0) for i in slow_steps]
    corner_steps = [(i, j) for i in slow_steps for j in fast_steps]
    plane = (rows, length)
    block_shape = (2, rows, length)
    piece_shape = (2, rows, LANES)
    matmul_cost = 2 * (2 * rows) * length * (2 * length) * 3
    chunks = range(per_facet)

    def window_scratch(count):
        return [
            pltpu.VMEM((count, 2, rows, length + LANES), jnp.float32),
            pltpu.SemaphoreType.DMA((count, blocks + 1)),
        ]

    last = per_facet - 1
    corner_keys = [(step, chunk) for step in corner_steps for chunk in chunks]
    near_keys = [(step, chunk) for chunk in chunks for step in [(0, 0)] + near_steps]

    def in_hbm(value):
        return pltpu.with_memory_space_constraint(value, pltpu.HBM)

    columns = in_hbm(facets)
    factor, *planes = call(
        functools.partial(corner_window_kernel, per_facet, near, corner_keys),
        [(subgrids, 2, length)] + [(per_facet, rows, length)] * (2 * len(corner_steps)),
        window_scratch(len(corner_keys))
        + [
            pltpu.SMEM(grid_offsets.shape, jnp.int32),
            pltpu.SMEM(facet_offsets.shape, jnp.int32),
            pltpu.VMEM((1, length), jnp.float32),
            pltpu.SemaphoreType.DMA((3,)),
        ],
        [HBM, HBM, HBM, HBM],
        8 * MIB,
        matmul_cost // 8,
    )(
        in_hbm(grid_offsets),
        in_hbm(facet_offsets),
        in_hbm(taper.reshape(1, length)),
        columns,
    )
    by_fast, by_slow = {}, {}
    for spot, (i, j) in enumerate(corner_steps):
        by_fast[i, j] = move(planes[2 * spot], 0, j)
        by_slow[i, j] = move(planes[2 * spot + 1], i, 0)

    near_layout = [2 if chunk == 0 and step != (0, 0) else 1 for step, chunk in near_keys]
    outs = call(
        functools.partial(window_kernel, near_layout, near, near_keys),
        [shape for count in near_layout for shape in ([block_shape], [plane] * 2)[count - 1]],
        window_scratch(len(near_keys)),
        [SMEM, HBM, VMEM],
        12 * MIB,
        matmul_cost // 4,
    )(grid_offsets, columns, factor)
    terms = {}
    for key, count in zip(near_keys, near_layout):
        terms[key], outs = tuple(outs[:count]), outs[count:]

    (chosen,) = call(
        choose_kernel, [residual.shape], [], [SMEM, VMEM], 4 * MIB, matmul_cost // 8
    )(kernel_index, kernels)

    def join(term, corners, part, chunk):
        if not corners:
            return term
        (joined,) = call(
            functools.partial(join_kernel, part, chunk, term.ndim == 3),
            [term.shape],
            [],
            [VMEM] * (1 + len(corners)),
            2 * MIB,
            matmul_cost // 64,
        )(term, *corners)
        return joined

    def scatter(chunk):
        received = [terms[(0, 0), chunk]]
        for i, j in near_steps:
            axis = SLOW if i else FAST
            part = 0 if i else 1
            if i:
                corners = [by_fast[i, j] for j in fast_steps]
            else:
                corners = [by_slow[i, j] for i in slow_steps]
            i, j = (i, 0) if axis == SLOW else (0, j)
            term = terms[(i, j), chunk]
            if len(term) == 1:
                joined = join(term[0], corners, part, chunk)
                received.append((move(joined, i, j),))
            else:
                early = move(term[1 - part], i, j)
                joined = join(term[part], corners, part, chunk)
                late = move(joined, i, j)
                received.append((late, early) if part == 0 else (early, late))
        return received

    def first_transform(received):
        arrays = [array for item in received for array in item]
        return call(
            functools.partial(first_kernel, [len(item) for item in received]),
            [piece_shape] * chips,
            [pltpu.VMEM(block_shape, jnp.float32)],
            [VMEM] + [VMEM] * len(arrays),
            8 * MIB,
            matmul_cost,
        )(table, *arrays)

    def cross(pieces, sign):
        return call(
            functools.partial(cross_kernel, sign),
            [block_shape] * 2,
            [
                pltpu.VMEM((2, chips * rows, LANES), jnp.float32),
                pltpu.VMEM((2, LANES, length), jnp.float32),
            ],
            [VMEM] + [VMEM] * chips,
            8 * MIB,
            matmul_cost,
        )(table, *pieces)

    def correct(keep, received, chunk):
        return call(
            functools.partial(correct_kernel, chunk),
            [piece_shape] * chips,
            [pltpu.VMEM(block_shape, jnp.float32)],
            [VMEM] * 5,
            8 * MIB,
            matmul_cost,
        )(table, keep, received, residual, chosen)

    def gather(own, chunk):
        found = {(0, 0): (own,)}
        split = chunk == last
        for i, j in near_steps:
            if split:
                part = 1 if i else 0
                early = move(own[part], i, j)
                late = move(own[1 - part], i, j)
                found[i, j] = (late, early) if part else (early, late)
            else:
                whole = move(own, i, j)
                found[i, j] = (whole,)

        def part_of(item, part):
            return item[part] if len(item) == 2 else item[0][part]

        for i, j in corner_steps:
            found[i, j] = (move(part_of(found[0, j], 0), i, 0), move(part_of(found[i, 0], 1), 0, j))
        return found

    received = [scatter(chunk) for chunk in chunks]
    pieces = [exchange(first_transform(received[chunk])) for chunk in chunks]
    halves = [cross(pieces[chunk], -1.0) for chunk in chunks]
    swapped = [swap(halves[chunk][1]) for chunk in chunks]
    pieces = [exchange(correct(halves[chunk][0], swapped[chunk], chunk)) for chunk in chunks]
    halves = [cross(pieces[chunk], 1.0) for chunk in chunks]
    keys, items = [], []
    for chunk in chunks:
        keep, sent = halves[chunk]
        own = keep + swap(sent)
        for (i, j), found in gather(own, chunk).items():
            keys.append(((-i, -j), chunk))
            items.append(found)
    *first_items, last_item = items
    if len(last_item) == 1:
        last_item = (last_item[0][0], last_item[0][1])
    arrays = [array for item in first_items for array in item]
    whole, window = call(
        functools.partial(update_kernel, [len(item) for item in first_items], near, keys),
        [(1, 2, rows, facet_len), (2, rows, length + LANES)],
        [],
        [SMEM, VMEM] + [VMEM] * len(arrays),
        16 * MIB,
        matmul_cost,
    )(grid_offsets, factor, *arrays)
    (update,) = call(
        functools.partial(finish_kernel, near, keys[-1]),
        [(1, 2, rows, facet_len)],
        [
            pltpu.VMEM((blocks + 1, 2, rows, LANES), jnp.float32),
            pltpu.SemaphoreType.DMA((blocks + 1,)),
        ],
        [SMEM, VMEM, VMEM, VMEM, VMEM, HBM],
        8 * MIB,
        matmul_cost // 8,
        out_specs=[HBM],
        input_output_aliases={5: 0},
    )(grid_offsets, factor, window, *last_item, whole)
    return update


def dft_tables(length):
    index = jnp.arange(length, dtype=jnp.int32)
    angle = (index[:, None] * index[None, :] % length).astype(jnp.float32) * (
        2.0 * math.pi / length
    )
    norm_scale = 1.0 / math.sqrt(length)
    return (jnp.cos(angle) * norm_scale, jnp.sin(angle) * norm_scale)


def transform_last(values, tables, sign):
    cosine, sine = tables
    real_part = values[:, 0]
    imag_part = values[:, 1]

    def multiply(left, right):
        return jnp.einsum("nab,bc->nac", left, right, precision=lax.Precision.HIGHEST)

    out_real = multiply(real_part, cosine) - sign * multiply(imag_part, sine)
    out_imag = multiply(imag_part, cosine) + sign * multiply(real_part, sine)
    return jnp.stack([out_real, out_imag], axis=1)


def plain_device(facets, facet_offsets, grid_offsets, taper, kernels, kernel_index, residual):
    columns = facets[0]
    length = taper.shape[0]
    facet_len = columns.shape[2]
    extended = jnp.concatenate([columns, columns[:, :, :length]], axis=2)
    facet_offset = facet_offsets[lax.axis_index("facet")]
    tables = dft_tables(length)

    def single(grid_offset):
        window = lax.dynamic_slice_in_dim(extended, window_start(grid_offset), length, 2)
        phase_real, phase_imag = phase_pair(facet_offset, grid_offset, length)
        factor_real = phase_real * taper
        factor_imag = phase_imag * taper
        return jnp.stack(
            [
                window[0] * factor_real - window[1] * factor_imag,
                window[0] * factor_imag + window[1] * factor_real,
            ]
        )

    terms = jax.vmap(single)(grid_offsets)
    summed = lax.psum_scatter(terms, "facet", scatter_dimension=0, tiled=True)
    summed = transform_last(summed, tables, -1.0)
    by_rows = lax.all_to_all(summed, "team", split_axis=3, concat_axis=2, tiled=True)
    by_rows = jnp.transpose(by_rows, (0, 1, 3, 2))
    spectrum = transform_last(by_rows, tables, -1.0)
    onehot = (kernel_index[:, :, None] == jnp.arange(kernels.shape[0], dtype=jnp.int32)).astype(
        jnp.float32
    )
    chosen = jnp.einsum("srk,kac->sarc", onehot, kernels, precision=lax.Precision.HIGHEST)
    corr_real = residual[:, 0] - (chosen[:, 0] * spectrum[:, 0] - chosen[:, 1] * spectrum[:, 1])
    corr_imag = residual[:, 1] - (chosen[:, 0] * spectrum[:, 1] + chosen[:, 1] * spectrum[:, 0])
    restored = transform_last(jnp.stack([corr_real, corr_imag], axis=1), tables, 1.0)
    restored = jnp.transpose(restored, (0, 1, 3, 2))
    by_columns = lax.all_to_all(restored, "team", split_axis=2, concat_axis=3, tiled=True)
    by_columns = transform_last(by_columns, tables, 1.0)
    initial = jnp.zeros(extended.shape, jnp.float32)
    piece = lax.all_gather(by_columns, "facet", axis=0, tiled=True)

    def add_one(item, total):
        grid_offset = grid_offsets[item]
        block = lax.dynamic_index_in_dim(piece, item, 0, keepdims=False)
        phase_real, phase_imag = phase_pair(facet_offset, grid_offset, length)
        value = jnp.stack(
            [
                (block[0] * phase_real + block[1] * phase_imag) * taper,
                (block[1] * phase_real - block[0] * phase_imag) * taper,
            ]
        )
        begin = window_start(grid_offset)
        current = lax.dynamic_slice_in_dim(total, begin, length, 2)
        return lax.dynamic_update_slice_in_dim(total, current + value, begin, 2)

    buffer = lax.fori_loop(0, piece.shape[0], add_one, initial)
    update = buffer[:, :, :facet_len].at[:, :, :length].add(buffer[:, :, facet_len:])
    return update[None]


def solution(mesh):
    facet_count, team_count = mesh.shape["facet"], mesh.shape["team"]

    def per_device(*arrays):
        rows, length, facet_len = arrays[0].shape[2], arrays[3].shape[0], arrays[0].shape[3]
        chips = team_count // 2
        tiled = (
            team_count % 2 == 0
            and chips & (chips - 1) == 0
            and 2 * rows == LANES
            and length == chips * LANES
            and facet_len % LANES == 0
            and arrays[6].shape[2] == rows
        )
        if tiled:
            return tiled_device(facet_count, team_count, *arrays)
        return plain_device(*arrays)

    return jax.shard_map(
        per_device,
        mesh=mesh,
        in_specs=(
            P("facet", None, "team", None),
            P(),
            P(),
            P(),
            P(),
            P("facet", "team"),
            P("facet", None, "team", None),
        ),
        out_specs=P("facet", None, "team", None),
        check_vma=False,
    )
```

```python
import functools
import math

import jax
import jax.numpy as jnp
import numpy as np
from jax import lax
from jax.experimental import pallas as pl
from jax.experimental.pallas import tpu as pltpu
from jax.sharding import PartitionSpec as P


N_IMG = 65536
FACET_LEN = 5120
LANES = 128
SLOW, FAST = range(2)


def mod_product(left, right):
    low_part = right % 256
    high_part = right // 256
    return (left * low_part + left * high_part % 256 * 256) % N_IMG


def window_start(grid_offset):
    return grid_offset * FACET_LEN // N_IMG


def phase_pair(facet_offset, grid_offset, length):
    position = (grid_offset + jnp.arange(length, dtype=jnp.int32)) % N_IMG
    angle = mod_product(facet_offset, position).astype(jnp.float32) * (2.0 * math.pi / N_IMG)
    return (jnp.cos(angle), jnp.sin(angle))


def split_table(length):
    index = np.arange(length)
    angle = (index[:, None] * index[None, :] % length) * (2.0 * np.pi / length)
    table = np.concatenate([np.cos(angle), np.sin(angle)], axis=1) / math.sqrt(length)
    high = table.astype(jnp.bfloat16)
    low = (table - high.astype(np.float64)).astype(jnp.bfloat16)
    return np.stack([high, low])


def product(values, high_table, low_table):
    high = values.astype(jnp.bfloat16)
    low = (values - high.astype(jnp.float32)).astype(jnp.bfloat16)

    def dot(left, right):
        return jnp.dot(left, right, preferred_element_type=jnp.float32)

    rows = values.shape[0]
    both = dot(jnp.concatenate([high, low], axis=0), high_table)
    return both[:rows] + (both[rows:] + dot(high, low_table))


def rotate(values, high_table, low_table, sign):
    rows = values.shape[0] // 2
    both = product(values, high_table, low_table)
    length = both.shape[1] // 2
    real = both[:rows, :length] - sign * both[rows:, length:]
    imag = both[rows:, :length] + sign * both[:rows, length:]
    return real, imag


def chip_and_core():
    team = lax.axis_index("team")
    return lax.div(team, 2), lax.rem(team, 2)


def lane_block(index):
    return pl.ds(pl.multiple_of(index * LANES, LANES), LANES)


def begin_of(offset):
    return lax.div(offset * FACET_LEN, N_IMG)


def phase_factor(offsets, facet_offset, taper, factor):
    count, _, length = factor.shape
    row = lax.broadcasted_iota(jnp.int32, (count, length), 0)
    position = lax.broadcasted_iota(jnp.int32, (count, length), 1)
    for item in range(count):
        position = position + jnp.where(row == item, offsets[item], 0)
    position = lax.bitwise_and(position, N_IMG - 1)
    low_part = lax.bitwise_and(position, 255)
    high_part = lax.shift_right_logical(position, 8)
    high_product = lax.bitwise_and(facet_offset * high_part, 255) * 256
    product = lax.bitwise_and(facet_offset * low_part + high_product, N_IMG - 1)
    angle = product.astype(jnp.float32) * (2.0 * math.pi / N_IMG)
    real = jnp.cos(angle) * taper
    imag = jnp.sin(angle) * taper
    for item in range(count):
        factor[item, 0:1, :] = real[item : item + 1, :]
        factor[item, 1:2, :] = imag[item : item + 1, :]


def pairs_of(layout, refs):
    refs = list(refs)
    pairs = []
    for planes in layout:
        if planes == 1:
            whole = refs.pop(0)
            pairs.append((whole.at[0], whole.at[1]))
        else:
            pairs.append((refs.pop(0), refs.pop(0)))
    return pairs


def cut_windows(offsets, ids, columns, outs, buffer, sems, prepare, factor):
    count = len(outs)
    total = columns.shape[3] // LANES
    blocks = factor.shape[2] // LANES

    def copy(item, piece):
        source = lax.rem(lax.div(begin_of(offsets[ids[item]]), LANES) + piece, total)
        return pltpu.make_async_copy(
            columns.at[0, :, :, lane_block(source)],
            buffer.at[item, :, :, pl.ds(piece * LANES, LANES)],
            sems.at[item, piece],
        )

    for item in range(count):
        for piece in range(blocks + 1):
            copy(item, piece).start()
    prepare()
    lane = lax.broadcasted_iota(jnp.int32, (columns.shape[2], LANES), 1)
    for item in range(count):
        for piece in range(blocks + 1):
            copy(item, piece).wait()
        shift = lax.rem(begin_of(offsets[ids[item]]), LANES)
        back = lax.rem(LANES - shift, LANES)
        keep = lane < LANES - shift
        for piece in range(blocks):
            span = pl.ds(piece * LANES, LANES)
            after = pl.ds((piece + 1) * LANES, LANES)
            parts = []
            for part in range(2):
                first = pltpu.roll(buffer[item, part, :, span], back, 1)
                second = pltpu.roll(buffer[item, part, :, after], back, 1)
                parts.append(jnp.where(keep, first, second))
            real, imag = parts
            factor_real = factor[ids[item], 0:1, span]
            factor_imag = factor[ids[item], 1:2, span]
            outs[item][0][:, span] = real * factor_real - imag * factor_imag
            outs[item][1][:, span] = real * factor_imag + imag * factor_real


def corner_window_kernel(
    per_facet, near, keys, offsets_hbm, facet_offsets_hbm, taper_hbm, columns, *refs
):
    factor, planes = refs[0], refs[1:-6]
    buffer, sems, offsets, facet_offsets, taper, small_sems = refs[-6:]
    small = [
        pltpu.make_async_copy(offsets_hbm, offsets, small_sems.at[0]),
        pltpu.make_async_copy(facet_offsets_hbm, facet_offsets, small_sems.at[1]),
        pltpu.make_async_copy(taper_hbm, taper, small_sems.at[2]),
    ]
    for copy in small:
        copy.start()
    small[0].wait()
    outs = [
        (planes[2 * step].at[chunk], planes[2 * step + 1].at[chunk])
        for step in range(len(planes) // 2)
        for chunk in range(per_facet)
    ]

    def prepare():
        small[1].wait()
        small[2].wait()
        phase_factor(offsets, facet_offsets[lax.axis_index("facet")], taper[...], factor)

    ids = [near(*key) for key in keys]
    cut_windows(offsets, ids, columns, outs, buffer, sems, prepare, factor)


def window_kernel(layout, near, keys, offsets, columns, factor, *refs):
    planes, (buffer, sems) = refs[:-2], refs[-2:]
    outs = pairs_of(layout, planes)
    ids = [near(*key) for key in keys]
    cut_windows(offsets, ids, columns, outs, buffer, sems, lambda: None, factor)


def join_kernel(part, chunk, whole, term, *refs):
    received, out = refs[:-1], refs[-1]
    if not whole:
        total = term[...]
    else:
        total = term[part]
        out[1 - part] = term[1 - part]
    for corner in received:
        total = total + corner[chunk]
    if whole:
        out[part] = total
    else:
        out[...] = total


def choose_kernel(index, kernels, out):
    chunks, _, rows, _ = out.shape
    for chunk in range(chunks):

        def step(row, carry):
            found = kernels[index[chunk, row]]
            out[chunk, 0, pl.ds(row, 1), :] = found[0:1]
            out[chunk, 1, pl.ds(row, 1), :] = found[1:2]
            return carry

        lax.fori_loop(0, rows, step, 0, unroll=8)


def split_out(values, outs):
    chip, _ = chip_and_core()
    for distance, out in enumerate(outs):
        out[...] = values[:, :, lane_block(jnp.bitwise_xor(chip, distance))]


def first_kernel(layout, table, *refs):
    scratch = refs[-1]
    chips = scratch.shape[2] // LANES
    terms, outs = refs[: -1 - chips], refs[-1 - chips : -1]
    pairs = pairs_of(layout, terms)
    sums = []
    for part in range(2):
        total = pairs[0][part][...]
        for pair in pairs[1:]:
            total = total + pair[part][...]
        sums.append(total)
    real, imag = rotate(jnp.concatenate(sums, axis=0), table[0], table[1], -1.0)
    scratch[0] = real
    scratch[1] = imag
    split_out(scratch, outs)


def cross_kernel(sign, table, *refs):
    blocks, (keep, send, gathered, partial) = refs[:-4], refs[-4:]
    chip, core = chip_and_core()
    rows = blocks[0].shape[1]
    for distance, block in enumerate(blocks):
        spot = pl.ds(pl.multiple_of(jnp.bitwise_xor(chip, distance) * rows, rows), rows)
        gathered[0, spot, :] = block[0]
        gathered[1, spot, :] = block[1]
    values = jnp.concatenate([gathered[0].T, gathered[1].T], axis=0)

    def own(half):
        pieces = [
            table[half, pl.ds(pl.multiple_of((2 * index + core) * rows, rows), rows), :]
            for index in range(len(blocks))
        ]
        return jnp.concatenate(pieces, axis=0)

    real, imag = rotate(values, own(0), own(1), sign)
    partial[0] = real
    partial[1] = imag
    mine = pl.ds(pl.multiple_of(core * rows, rows), rows)
    other = pl.ds(pl.multiple_of((1 - core) * rows, rows), rows)
    keep[...] = partial[:, mine, :]
    send[...] = partial[:, other, :]


def correct_kernel(chunk, table, keep, received, residuals, chosens, *refs):
    outs, scratch = refs[:-1], refs[-1]
    residual, chosen = residuals.at[chunk], chosens.at[chunk]
    spectrum_real = keep[0] + received[0]
    spectrum_imag = keep[1] + received[1]
    real = residual[0] - (chosen[0] * spectrum_real - chosen[1] * spectrum_imag)
    imag = residual[1] - (chosen[0] * spectrum_imag + chosen[1] * spectrum_real)
    values = jnp.concatenate([real, imag], axis=0)
    real, imag = rotate(values, table[0], table[1], 1.0)
    scratch[0] = real
    scratch[1] = imag
    split_out(scratch, outs)


def turned_pieces(offset, factor, real_ref, imag_ref):
    rows, length = real_ref.shape
    blocks = length // LANES
    begin = begin_of(offset)
    shift = lax.rem(begin, LANES)
    lane = lax.broadcasted_iota(jnp.int32, (rows, LANES), 1)
    late = lane >= shift
    empty = jnp.zeros((rows, LANES), jnp.float32)
    earlier = [empty, empty]
    pieces = []
    for piece in range(blocks + 1):
        turned = [empty, empty]
        if piece < blocks:
            span = pl.ds(piece * LANES, LANES)
            real, imag = real_ref[:, span], imag_ref[:, span]
            factor_real, factor_imag = factor[0:1, span], factor[1:2, span]
            turned = [
                pltpu.roll(real * factor_real + imag * factor_imag, shift, 1),
                pltpu.roll(imag * factor_real - real * factor_imag, shift, 1),
            ]
        pieces.append([jnp.where(late, turned[part], earlier[part]) for part in range(2)])
        earlier = turned
    return lax.div(begin, LANES), pieces


def update_kernel(layout, near, keys, offsets, factor, *refs):
    arrays, (out, window) = refs[:-2], refs[-2:]
    pairs = pairs_of(layout, arrays)
    ids = [near(*key) for key in keys]
    count = len(pairs)
    total = out.shape[3] // LANES
    out[...] = jnp.zeros(out.shape, jnp.float32)
    for item in range(count):
        block, pieces = turned_pieces(
            offsets[ids[item]], factor.at[ids[item]], *pairs[item]
        )
        for piece, parts in enumerate(pieces):
            spot = lane_block(lax.rem(block + piece, total))
            for part in range(2):
                out[0, part, :, spot] += parts[part]
    block = lax.div(begin_of(offsets[ids[count]]), LANES)
    for piece in range(window.shape[2] // LANES):
        spot = lane_block(lax.rem(block + piece, total))
        window[:, :, pl.ds(piece * LANES, LANES)] = out[0, :, :, spot]


def finish_kernel(near, key, offsets, factor, window, real, imag, whole, out, buffer, sems):
    total = out.shape[3] // LANES
    item = near(*key)
    spot = lax.broadcasted_iota(jnp.int32, offsets.shape, 1)
    offset = jnp.sum(jnp.where(spot == item, offsets[...], 0))
    block, pieces = turned_pieces(offset, factor.at[item], real, imag)

    def copy(piece):
        return pltpu.make_async_copy(
            buffer.at[piece],
            out.at[0, :, :, lane_block(lax.rem(block + piece, total))],
            sems.at[piece],
        )

    for piece, parts in enumerate(pieces):
        span = pl.ds(piece * LANES, LANES)
        for part in range(2):
            buffer[piece, part] = window[part, :, span] + parts[part]
        copy(piece).start()
    for piece in range(len(pieces)):
        copy(piece).wait()


VMEM = pl.BlockSpec(memory_space=pltpu.VMEM)
SMEM = pl.BlockSpec(memory_space=pltpu.SMEM)
HBM = pl.BlockSpec(memory_space=pltpu.HBM)
MIB = 1 << 20


def call(kernel, outs, scratch, specs, limit, cost, **kwargs):
    return pl.pallas_call(
        kernel,
        out_shape=[jax.ShapeDtypeStruct(shape, jnp.float32) for shape in outs],
        in_specs=specs,
        out_specs=kwargs.pop("out_specs", [VMEM] * len(outs)),
        scratch_shapes=scratch,
        compiler_params=pltpu.CompilerParams(vmem_limit_bytes=limit),
        cost_estimate=pl.CostEstimate(flops=cost, bytes_accessed=cost // 64, transcendentals=0),
        **kwargs,
    )


def jump_order(chips):
    return list(range(chips - 1, 0, -1))


def grid_of(count):
    slow = max(step for step in range(1, math.isqrt(count) + 1) if count % step == 0)
    return slow, count // slow


def tiled_device(
    facet_count, team_count, facets, facet_offsets, grid_offsets, taper, kernels, kernel_index, residual
):
    rows = facets.shape[2]
    length = taper.shape[0]
    facet_len = facets.shape[3]
    blocks = length // LANES
    chips = team_count // 2
    per_facet = residual.shape[0]
    subgrids = grid_offsets.shape[0]
    slow, fast = grid_of(facet_count)
    table = jnp.asarray(split_table(length))

    def near(step, chunk):
        facet = lax.axis_index("facet")
        down, right = lax.div(facet, fast), lax.rem(facet, fast)
        to = lax.rem(down + step[0] % slow, slow) * fast + lax.rem(right + step[1] % fast, fast)
        return to * per_facet + chunk

    def move(value, step_slow, step_fast):
        pairs = [
            (
                spot,
                (spot // fast + step_slow) % slow * fast + (spot % fast + step_fast) % fast,
            )
            for spot in range(facet_count)
        ]
        return lax.ppermute(value, "facet", pairs)

    def exchange(pieces):
        out = [pieces[0]] + [None] * (chips - 1)
        for distance in jump_order(chips):
            pairs = [
                (spot, (spot // 2 ^ distance) * 2 + spot % 2) for spot in range(team_count)
            ]
            out[distance] = lax.ppermute(pieces[distance], "team", pairs)
        return out

    def swap(value):
        return lax.ppermute(value, "team", [(spot, spot ^ 1) for spot in range(team_count)])

    slow_steps, fast_steps = range(1, slow), range(1, fast)
    near_steps = [(0, j) for j in fast_steps] + [(i, 0) for i in slow_steps]
    corner_steps = [(i, j) for i in slow_steps for j in fast_steps]
    plane = (rows, length)
    block_shape = (2, rows, length)
    piece_shape = (2, rows, LANES)
    matmul_cost = 2 * (2 * rows) * length * (2 * length) * 3
    chunks = range(per_facet)

    def window_scratch(count):
        return [
            pltpu.VMEM((count, 2, rows, length + LANES), jnp.float32),
            pltpu.SemaphoreType.DMA((count, blocks + 1)),
        ]

    last = per_facet - 1
    corner_keys = [(step, chunk) for step in corner_steps for chunk in chunks]
    near_keys = [(step, chunk) for chunk in chunks for step in [(0, 0)] + near_steps]

    def in_hbm(value):
        return pltpu.with_memory_space_constraint(value, pltpu.HBM)

    columns = in_hbm(facets)
    factor, *planes = call(
        functools.partial(corner_window_kernel, per_facet, near, corner_keys),
        [(subgrids, 2, length)] + [(per_facet, rows, length)] * (2 * len(corner_steps)),
        window_scratch(len(corner_keys))
        + [
            pltpu.SMEM(grid_offsets.shape, jnp.int32),
            pltpu.SMEM(facet_offsets.shape, jnp.int32),
            pltpu.VMEM((1, length), jnp.float32),
            pltpu.SemaphoreType.DMA((3,)),
        ],
        [HBM, HBM, HBM, HBM],
        8 * MIB,
        matmul_cost // 8,
    )(
        in_hbm(grid_offsets),
        in_hbm(facet_offsets),
        in_hbm(taper.reshape(1, length)),
        columns,
    )
    by_fast, by_slow = {}, {}
    for spot, (i, j) in enumerate(corner_steps):
        by_fast[i, j] = move(planes[2 * spot], 0, j)
        by_slow[i, j] = move(planes[2 * spot + 1], i, 0)

    near_layout = [2 if chunk == 0 and step != (0, 0) else 1 for step, chunk in near_keys]
    outs = call(
        functools.partial(window_kernel, near_layout, near, near_keys),
        [shape for count in near_layout for shape in ([block_shape], [plane] * 2)[count - 1]],
        window_scratch(len(near_keys)),
        [SMEM, HBM, VMEM],
        12 * MIB,
        matmul_cost // 4,
    )(grid_offsets, columns, factor)
    terms = {}
    for key, count in zip(near_keys, near_layout):
        terms[key], outs = tuple(outs[:count]), outs[count:]

    (chosen,) = call(
        choose_kernel, [residual.shape], [], [SMEM, VMEM], 4 * MIB, matmul_cost // 8
    )(kernel_index, kernels)

    def join(term, corners, part, chunk):
        if not corners:
            return term
        (joined,) = call(
            functools.partial(join_kernel, part, chunk, term.ndim == 3),
            [term.shape],
            [],
            [VMEM] * (1 + len(corners)),
            2 * MIB,
            matmul_cost // 64,
        )(term, *corners)
        return joined

    def scatter(chunk):
        received = [terms[(0, 0), chunk]]
        for i, j in near_steps:
            axis = SLOW if i else FAST
            part = 0 if i else 1
            if i:
                corners = [by_fast[i, j] for j in fast_steps]
            else:
                corners = [by_slow[i, j] for i in slow_steps]
            i, j = (i, 0) if axis == SLOW else (0, j)
            term = terms[(i, j), chunk]
            if len(term) == 1:
                joined = join(term[0], corners, part, chunk)
                received.append((move(joined, i, j),))
            else:
                early = move(term[1 - part], i, j)
                joined = join(term[part], corners, part, chunk)
                late = move(joined, i, j)
                received.append((late, early) if part == 0 else (early, late))
        return received

    def first_transform(received):
        arrays = [array for item in received for array in item]
        return call(
            functools.partial(first_kernel, [len(item) for item in received]),
            [piece_shape] * chips,
            [pltpu.VMEM(block_shape, jnp.float32)],
            [VMEM] + [VMEM] * len(arrays),
            8 * MIB,
            matmul_cost,
        )(table, *arrays)

    def cross(pieces, sign):
        return call(
            functools.partial(cross_kernel, sign),
            [block_shape] * 2,
            [
                pltpu.VMEM((2, chips * rows, LANES), jnp.float32),
                pltpu.VMEM((2, LANES, length), jnp.float32),
            ],
            [VMEM] + [VMEM] * chips,
            8 * MIB,
            matmul_cost,
        )(table, *pieces)

    def correct(keep, received, chunk):
        return call(
            functools.partial(correct_kernel, chunk),
            [piece_shape] * chips,
            [pltpu.VMEM(block_shape, jnp.float32)],
            [VMEM] * 5,
            8 * MIB,
            matmul_cost,
        )(table, keep, received, residual, chosen)

    def gather(own, chunk):
        found = {(0, 0): (own,)}
        split = chunk == last
        for i, j in near_steps:
            if split:
                part = 1 if i else 0
                early = move(own[part], i, j)
                late = move(own[1 - part], i, j)
                found[i, j] = (late, early) if part else (early, late)
            else:
                whole = move(own, i, j)
                found[i, j] = (whole,)

        def part_of(item, part):
            return item[part] if len(item) == 2 else item[0][part]

        for i, j in corner_steps:
            found[i, j] = (move(part_of(found[0, j], 0), i, 0), move(part_of(found[i, 0], 1), 0, j))
        return found

    received = [scatter(chunk) for chunk in chunks]
    pieces = [exchange(first_transform(received[chunk])) for chunk in chunks]
    halves = [cross(pieces[chunk], -1.0) for chunk in chunks]
    swapped = [swap(halves[chunk][1]) for chunk in chunks]
    pieces = [exchange(correct(halves[chunk][0], swapped[chunk], chunk)) for chunk in chunks]
    halves = [cross(pieces[chunk], 1.0) for chunk in chunks]
    keys, items = [], []
    for chunk in chunks:
        keep, sent = halves[chunk]
        own = keep + swap(sent)
        for (i, j), found in gather(own, chunk).items():
            keys.append(((-i, -j), chunk))
            items.append(found)
    *first_items, last_item = items
    if len(last_item) == 1:
        last_item = (last_item[0][0], last_item[0][1])
    arrays = [array for item in first_items for array in item]
    whole, window = call(
        functools.partial(update_kernel, [len(item) for item in first_items], near, keys),
        [(1, 2, rows, facet_len), (2, rows, length + LANES)],
        [],
        [SMEM, VMEM] + [VMEM] * len(arrays),
        16 * MIB,
        matmul_cost,
    )(grid_offsets, factor, *arrays)
    (update,) = call(
        functools.partial(finish_kernel, near, keys[-1]),
        [(1, 2, rows, facet_len)],
        [
            pltpu.VMEM((blocks + 1, 2, rows, LANES), jnp.float32),
            pltpu.SemaphoreType.DMA((blocks + 1,)),
        ],
        [VMEM] * 5 + [HBM],
        8 * MIB,
        matmul_cost // 8,
        out_specs=[HBM],
        input_output_aliases={5: 0},
    )(grid_offsets.reshape(1, subgrids), factor, window, *last_item, whole)
    return update


def dft_tables(length):
    index = jnp.arange(length, dtype=jnp.int32)
    angle = (index[:, None] * index[None, :] % length).astype(jnp.float32) * (
        2.0 * math.pi / length
    )
    norm_scale = 1.0 / math.sqrt(length)
    return (jnp.cos(angle) * norm_scale, jnp.sin(angle) * norm_scale)


def transform_last(values, tables, sign):
    cosine, sine = tables
    real_part = values[:, 0]
    imag_part = values[:, 1]

    def multiply(left, right):
        return jnp.einsum("nab,bc->nac", left, right, precision=lax.Precision.HIGHEST)

    out_real = multiply(real_part, cosine) - sign * multiply(imag_part, sine)
    out_imag = multiply(imag_part, cosine) + sign * multiply(real_part, sine)
    return jnp.stack([out_real, out_imag], axis=1)


def plain_device(facets, facet_offsets, grid_offsets, taper, kernels, kernel_index, residual):
    columns = facets[0]
    length = taper.shape[0]
    facet_len = columns.shape[2]
    extended = jnp.concatenate([columns, columns[:, :, :length]], axis=2)
    facet_offset = facet_offsets[lax.axis_index("facet")]
    tables = dft_tables(length)

    def single(grid_offset):
        window = lax.dynamic_slice_in_dim(extended, window_start(grid_offset), length, 2)
        phase_real, phase_imag = phase_pair(facet_offset, grid_offset, length)
        factor_real = phase_real * taper
        factor_imag = phase_imag * taper
        return jnp.stack(
            [
                window[0] * factor_real - window[1] * factor_imag,
                window[0] * factor_imag + window[1] * factor_real,
            ]
        )

    terms = jax.vmap(single)(grid_offsets)
    summed = lax.psum_scatter(terms, "facet", scatter_dimension=0, tiled=True)
    summed = transform_last(summed, tables, -1.0)
    by_rows = lax.all_to_all(summed, "team", split_axis=3, concat_axis=2, tiled=True)
    by_rows = jnp.transpose(by_rows, (0, 1, 3, 2))
    spectrum = transform_last(by_rows, tables, -1.0)
    onehot = (kernel_index[:, :, None] == jnp.arange(kernels.shape[0], dtype=jnp.int32)).astype(
        jnp.float32
    )
    chosen = jnp.einsum("srk,kac->sarc", onehot, kernels, precision=lax.Precision.HIGHEST)
    corr_real = residual[:, 0] - (chosen[:, 0] * spectrum[:, 0] - chosen[:, 1] * spectrum[:, 1])
    corr_imag = residual[:, 1] - (chosen[:, 0] * spectrum[:, 1] + chosen[:, 1] * spectrum[:, 0])
    restored = transform_last(jnp.stack([corr_real, corr_imag], axis=1), tables, 1.0)
    restored = jnp.transpose(restored, (0, 1, 3, 2))
    by_columns = lax.all_to_all(restored, "team", split_axis=2, concat_axis=3, tiled=True)
    by_columns = transform_last(by_columns, tables, 1.0)
    initial = jnp.zeros(extended.shape, jnp.float32)
    piece = lax.all_gather(by_columns, "facet", axis=0, tiled=True)

    def add_one(item, total):
        grid_offset = grid_offsets[item]
        block = lax.dynamic_index_in_dim(piece, item, 0, keepdims=False)
        phase_real, phase_imag = phase_pair(facet_offset, grid_offset, length)
        value = jnp.stack(
            [
                (block[0] * phase_real + block[1] * phase_imag) * taper,
                (block[1] * phase_real - block[0] * phase_imag) * taper,
            ]
        )
        begin = window_start(grid_offset)
        current = lax.dynamic_slice_in_dim(total, begin, length, 2)
        return lax.dynamic_update_slice_in_dim(total, current + value, begin, 2)

    buffer = lax.fori_loop(0, piece.shape[0], add_one, initial)
    update = buffer[:, :, :facet_len].at[:, :, :length].add(buffer[:, :, facet_len:])
    return update[None]


def solution(mesh):
    facet_count, team_count = mesh.shape["facet"], mesh.shape["team"]

    def per_device(*arrays):
        rows, length, facet_len = arrays[0].shape[2], arrays[3].shape[0], arrays[0].shape[3]
        chips = team_count // 2
        tiled = (
            team_count % 2 == 0
            and chips & (chips - 1) == 0
            and 2 * rows == LANES
            and length == chips * LANES
            and facet_len % LANES == 0
            and arrays[6].shape[2] == rows
        )
        if tiled:
            return tiled_device(facet_count, team_count, *arrays)
        return plain_device(*arrays)

    return jax.shard_map(
        per_device,
        mesh=mesh,
        in_specs=(
            P("facet", None, "team", None),
            P(),
            P(),
            P(),
            P(),
            P("facet", "team"),
            P("facet", None, "team", None),
        ),
        out_specs=P("facet", None, "team", None),
        check_vma=False,
    )
```
